32 devices in a mesh: row: 16 (over z, y, x), col: 2 (over core).
Axes of the slice: x: 2, y: 2, z: 4, core: 2. Of those that a mesh axis runs over, the one named last changes fastest.
Arguments:
- offsets: float32 [2, 32768], P(None, ('row', 'col')), may hold values from 0 to 1
- site_cell: int32 [32768], P(('row', 'col')), may hold values from 0 to 511, as said below
- estimates: float32 [4, 64, 8], P(None, 'row', 'col'), may hold values from -0.7 to 0.7
- panel_tile: int32 [1], replicated, may hold values from 0 to 63
Outputs:
- panel: float32 [512, 32768], P('col', 'row')
- fields: float32 [4, 32768], P(None, ('row', 'col'))
The draws below stay inside these ranges and needn't reach their ends.
Inputs may be any that keep to these rules, and one draw needn't show every extreme that they name: `site_cell`: the site with global index g lies on device number g // 1024 of the row-major (row) by (col) grid of devices; for device (r, c) its cell's first index lies in r * 4 to r * 4 + 3 and its second index in c * 4 to c * 4 + 3.
All inputs are finite; a program needn't handle non-finite values.
Results may differ from the reference program's by a relative error of at most 0.0003.
Values sent between devices are 32-bit elements; how exact they have to be, the bound alone decides.
No kernel may reach another device: no remote copies, remote signals or barrier semaphores. Data moves between devices by JAX's collectives and lax.ppermute only.
A program may use at most 64 MiB of HBM per device.

```python
import jax
import jax.numpy as jnp
from jax import lax

SITE_DEV = 1024
TILE = 512
CELL_X = 4
CELL_Y = 4
RADIUS = 2
GX = 64
GY = 8
SITES = 32768
N_COL = 2


def draw_site_cell(key, part):
    index = jnp.arange(SITES, dtype=jnp.int32)
    device = index // SITE_DEV
    block_x = device // N_COL
    block_y = device % N_COL
    local = jax.random.randint(key, (SITES,), 0, CELL_X * CELL_Y, dtype=jnp.int32)
    cell_x = block_x * CELL_X + local // CELL_Y
    cell_y = block_y * CELL_Y + local % CELL_Y
    return (cell_x * GY + cell_y).astype(jnp.int32)


def level_of(key, dims, cuts, smallest, high):
    level, own = 1.0, jax.random.fold_in(key, 6)
    for position, parts in cuts:
        draws = jnp.exp(jax.random.uniform(jax.random.fold_in(own, position), (parts,), jnp.float32, smallest / len(cuts), high / len(cuts)))
        level = level * jnp.repeat(draws, dims[position] // parts).reshape([-1 if axis == position else 1 for axis in range(len(dims))])
    return level


def setup_inputs(seed: int = 0) -> dict:
    arg_keys = jax.random.split(jax.random.key(seed), 5)
    offsets = jnp.clip(1.0 * jax.random.uniform(arg_keys[0], (2, SITES), jnp.float32) ** level_of(arg_keys[0], (2, SITES), ((1, 32),), -0.2, 0.2), 0.0, 1.0)
    site_cell = draw_site_cell(jax.random.fold_in(arg_keys[4], 71), 0)
    estimates = jnp.clip(jax.random.uniform(arg_keys[2], (4, GX, GY), jnp.float32, -0.7, 0.7) * level_of(arg_keys[2], (4, GX, GY), ((1, 16), (2, 2)), -0.4, 0.0), -0.7, 0.7)
    panel_tile = jax.random.randint(arg_keys[3], (1,), 0, SITES // TILE).astype(jnp.int32)
    return {"offsets": offsets, "site_cell": site_cell, "estimates": estimates, "panel_tile": panel_tile}


spread_cells = 1.5
nugget_share = 0.5
range_shift = -0.7

def profile(start, count, total, cells, loc):
    coord = start + jnp.arange(count, dtype=jnp.int32)
    inside = (coord[:, None] >= 0) & (coord[:, None] < total) & (jnp.abs(coord[:, None] - cells[None, :]) <= RADIUS)
    dist = loc[None, :] - coord[:, None].astype(jnp.float32) - 0.5
    return jnp.where(inside, jnp.exp(-dist * dist / (2.0 * spread_cells * spread_cells)), jnp.float32(0.0))

def smooth(window, start_x, start_y, total_x, total_y, offsets, site_cell, grid_y):
    cell_x = site_cell // grid_y
    cell_y = site_cell % grid_y
    loc_x = cell_x.astype(jnp.float32) + offsets[0]
    loc_y = cell_y.astype(jnp.float32) + offsets[1]
    weight_x = profile(start_x, window.shape[1], total_x, cell_x, loc_x)
    weight_y = profile(start_y, window.shape[2], total_y, cell_y, loc_y)
    partial_sums = jnp.einsum('fab,bs->fas', window, weight_y, precision=lax.Precision.HIGHEST)
    numer = lax.optimization_barrier(jnp.sum(partial_sums * weight_x[None], axis=1))
    denom = lax.optimization_barrier(jnp.sum(weight_x, axis=0)) * lax.optimization_barrier(jnp.sum(weight_y, axis=0))
    return (numer / denom, jnp.stack([loc_x, loc_y]))

def sigma_terms(data):
    first = jnp.exp(2.0 * (data[0] + range_shift))
    second = jnp.exp(2.0 * (data[1] + range_shift))
    cosine = jnp.cos(data[2])
    sine = jnp.sin(data[2])
    return (cosine * cosine * first + sine * sine * second, sine * sine * first + cosine * cosine * second, cosine * sine * (first - second), data[0] + data[1] + 2.0 * range_shift)

def covariance(rows, cols, same):
    row_a, row_b, row_c, row_l = sigma_terms(rows)
    col_a, col_b, col_c, col_l = sigma_terms(cols)
    m_aa = 0.5 * (row_a[:, None] + col_a[None, :])
    m_bb = 0.5 * (row_b[:, None] + col_b[None, :])
    m_ab = 0.5 * (row_c[:, None] + col_c[None, :])
    det_m = m_aa * m_bb - m_ab * m_ab
    diff_x = rows[4][:, None] - cols[4][None, :]
    diff_y = rows[5][:, None] - cols[5][None, :]
    quad = (m_bb * diff_x * diff_x - 2.0 * m_ab * diff_x * diff_y + m_aa * diff_y * diff_y) / det_m
    dist = jnp.sqrt(3.0 * jnp.maximum(quad, 0.0))
    scale = jnp.exp(rows[3][:, None] + cols[3][None, :] + 0.5 * (row_l[:, None] + col_l[None, :]))
    value = scale / jnp.sqrt(det_m) * (1.0 + dist) * jnp.exp(-dist)
    return value + jnp.where(same, nugget_share * jnp.exp(2.0 * rows[3])[:, None], jnp.float32(0.0))

def reference(offsets, site_cell, estimates, panel_tile):
    fields, loc = smooth(estimates, 0, 0, GX, GY, offsets, site_cell, GY)
    data = jnp.concatenate([fields, loc / GX], axis=0)
    start = panel_tile[0] * TILE
    piece = lax.dynamic_slice_in_dim(data, start, TILE, 1)
    cols_index = start + jnp.arange(TILE, dtype=jnp.int32)
    eye = jnp.arange(TILE)[:, None] == jnp.arange(TILE)[None, :]
    factor = jnp.linalg.cholesky(covariance(piece, piece, eye))
    count = SITES // TILE
    blocks = data.reshape(6, count, TILE).transpose(1, 0, 2)

    def solve_block(args):
        block, number = args
        rows_index = number * TILE + jnp.arange(TILE, dtype=jnp.int32)
        matrix = covariance(piece, block, cols_index[:, None] == rows_index[None, :])
        return jax.scipy.linalg.solve_triangular(factor, matrix, lower=True)
    panel = lax.map(solve_block, (blocks, jnp.arange(count, dtype=jnp.int32)))
    return (panel.transpose(1, 0, 2).reshape(TILE, SITES), fields)
```

```python
import functools

import jax
import jax.numpy as jnp
from jax import lax
from jax.experimental import pallas as pl
from jax.experimental.pallas import tpu as pltpu
from jax.sharding import PartitionSpec as P

SITE_DEV = 1024
TILE = 512
CELL_X = 4
CELL_Y = 4
RADIUS = 2

spread_cells = 1.5
nugget_share = 0.5
range_shift = -0.7

LANES = 128
BLOCK = 128
FIELDS = 4
SITE_ROWS = SITE_DEV // LANES
TILE_ROWS = TILE // LANES
HEAD = 3 * TILE_ROWS
CHUNK = 256
QUANT = 6

HIGHEST = lax.Precision.HIGHEST


def dot(a, b):
    return jnp.dot(a, b, precision=HIGHEST, preferred_element_type=jnp.float32)


def dot_t(a, b):
    return lax.dot_general(
        a, b, (((1,), (1,)), ((), ())), precision=HIGHEST, preferred_element_type=jnp.float32
    )


def pack_kernel(cols, tile_ref, est_ref, offsets_ref, cell_ref, raw_ref, buf_ref):
    row = lax.axis_index("row")
    col = lax.axis_index("col")
    for j in range(SITE_ROWS):
        part = slice(j * LANES, (j + 1) * LANES)
        raw_ref[j : j + 1, :] = offsets_ref[0:1, part]
        raw_ref[SITE_ROWS + j : SITE_ROWS + j + 1, :] = offsets_ref[1:2, part]
        raw_ref[2 * SITE_ROWS + j : 2 * SITE_ROWS + j + 1, :] = cell_ref[0:1, part].astype(
            jnp.float32
        )
    start = tile_ref[0] * TILE
    root = start // SITE_DEV
    first = (start - root * SITE_DEV) // LANES
    mine = row * cols + col == root
    for q in range(3):
        rows = raw_ref[pl.ds(q * SITE_ROWS + first, TILE_ROWS), :]
        buf_ref[q * TILE_ROWS : (q + 1) * TILE_ROWS, :] = jnp.where(mine, rows, 0.0)
    grid_y = cols * CELL_Y
    lane = lax.broadcasted_iota(jnp.int32, (1, LANES), 1) - col * CELL_Y
    line = jnp.zeros((1, LANES), jnp.float32)
    for f in range(FIELDS):
        for a in range(CELL_X):
            for b in range(CELL_Y):
                line = jnp.where(
                    lane == (f * CELL_X + a) * grid_y + b, est_ref[f, a, b], line
                )
    count = buf_ref.shape[0] - HEAD
    index = lax.broadcasted_iota(jnp.int32, (count, LANES), 0)
    buf_ref[HEAD:, :] = jnp.where(index == row, jnp.broadcast_to(line, (count, LANES)), 0.0)


def smooth(raw, block_row, table_ref, rows_mesh, grid_y):
    off_x, off_y, cell = raw
    total_x = CELL_X * rows_mesh
    cell_x = jnp.floor((cell + 0.5) / grid_y)
    cell_y = cell - cell_x * grid_y
    loc_x = cell_x + off_x
    loc_y = cell_y + off_y
    weight_y = []
    for b in range(grid_y):
        dist = loc_y - (b + 0.5)
        value = jnp.exp(-dist * dist / (2.0 * spread_cells * spread_cells))
        weight_y.append(jnp.where(jnp.abs(cell_y - b) <= RADIUS, value, 0.0))
    sum_y = functools.reduce(jnp.add, weight_y)
    numer = [None] * FIELDS
    sum_x = None
    for a in range(CELL_X - RADIUS, 2 * CELL_X + RADIUS):
        coord = (block_row - 1) * CELL_X + a
        near = block_row - 1 + a // CELL_X
        line = HEAD + jnp.clip(near, 0, rows_mesh - 1)
        coord_f = coord.astype(jnp.float32)
        dist = loc_x - coord_f - 0.5
        value = jnp.exp(-dist * dist / (2.0 * spread_cells * spread_cells))
        inside = (coord >= 0) & (coord < total_x)
        reach = jnp.where(inside, float(RADIUS), -1.0)
        weight = jnp.where(jnp.abs(cell_x - coord_f) <= reach, value, 0.0)
        sum_x = weight if sum_x is None else sum_x + weight
        for f in range(FIELDS):
            base = (f * CELL_X + a % CELL_X) * grid_y
            inner = None
            for b in range(grid_y):
                term = table_ref[line, base + b] * weight_y[b]
                inner = term if inner is None else inner + term
            term = inner * weight
            numer[f] = term if numer[f] is None else numer[f] + term
    denom = sum_x * sum_y
    return [n / denom for n in numer], loc_x, loc_y


def quantities(fields, loc_x, loc_y, total_x):
    first = jnp.exp(2.0 * (fields[0] + range_shift))
    second = jnp.exp(2.0 * (fields[1] + range_shift))
    cosine = jnp.cos(fields[2])
    sine = jnp.sin(fields[2])
    half_a = 0.5 * (cosine * cosine * first + sine * sine * second)
    half_b = 0.5 * (sine * sine * first + cosine * cosine * second)
    half_c = 0.5 * (cosine * sine * (first - second))
    scale = jnp.exp(fields[3] + 0.5 * (fields[0] + fields[1] + 2.0 * range_shift))
    return [half_a, half_b, half_c, loc_x / total_x, loc_y / total_x, scale]


def covariance(cols, rows):
    m_aa = cols[0] + rows[0]
    m_bb = cols[1] + rows[1]
    m_ab = cols[2] + rows[2]
    diff_x = cols[3] - rows[3]
    diff_y = cols[4] - rows[4]
    inv_root = lax.rsqrt(m_aa * m_bb - m_ab * m_ab)
    form = diff_x * (m_bb * diff_x - m_ab * diff_y) + diff_y * (m_aa * diff_y - m_ab * diff_x)
    square = jnp.maximum(form * (3.0 * inv_root * inv_root), 1e-36)
    dist = square * lax.rsqrt(square)
    return (cols[5] * rows[5]) * inv_root * (1.0 + dist) * jnp.exp(-dist)


def lane_copy(values, lane):
    index = jnp.full(values.shape, lane, jnp.int32)
    return jnp.take_along_axis(values, index, axis=1)


def row_copy(values, row):
    return jnp.broadcast_to(values[row : row + 1, :], values.shape)


def inverse_factor(rows):
    steps = BLOCK // 8
    lane = lax.broadcasted_iota(jnp.int32, (8, BLOCK), 1)
    sub = lax.broadcasted_iota(jnp.int32, (8, BLOCK), 0)
    rows = list(rows)
    out = [None] * steps
    for m in range(steps):
        at = 8 * m
        pivots = (lane >= at) & (lane < at + 8)
        column = [lane_copy(rows[m], at + c) for c in range(8)]
        block = jnp.where(lane - at == sub, 1.0, jnp.where(pivots, 0.0, rows[m]))
        solved = None
        inverse = None
        for c in range(8):
            pivot = row_copy(column[c], c)
            inv = 1.0 / pivot
            line = row_copy(block, c)
            scaled = line * lax.rsqrt(pivot)
            solved = scaled if c == 0 else jnp.where(sub == c, scaled, solved)
            inverse = inv if c == 0 else jnp.where(sub == c, inv, inverse)
            others = jnp.where(sub == c, 0.0, column[c])
            for j in range(c + 1, 8):
                column[j] = column[j] - (others * row_copy(column[j], c)) * inv
            block = block - (others * line) * inv
        out[m] = solved
        if m == steps - 1:
            break
        block = block * inverse
        lines = [row_copy(block, c) for c in range(8)]
        for i in range(m + 1, steps):
            p = [lane_copy(rows[i], at + c) * lines[c] for c in range(8)]
            total = ((p[0] + p[1]) + (p[2] + p[3])) + ((p[4] + p[5]) + (p[6] + p[7]))
            rows[i] = jnp.where(pivots, 0.0, rows[i]) - total
    result = jnp.concatenate(out, axis=0)
    r = lax.broadcasted_iota(jnp.int32, (BLOCK, BLOCK), 0)
    c = lax.broadcasted_iota(jnp.int32, (BLOCK, BLOCK), 1)
    return jnp.where(c <= r, result, 0.0)


def at(block):
    return slice(block * BLOCK, (block + 1) * BLOCK)


def main_kernel(
    rows_mesh, cols, tile_ref, table_ref, buf_ref, *refs
):
    raws = refs[:cols]
    panel_ref, fields_ref, colq, rowq, siteq, gram, inv, solved, cov, sems = refs[cols:]
    row = lax.axis_index("row")
    col = lax.axis_index("col")
    grid_y = cols * CELL_Y
    total_x = float(CELL_X * rows_mesh)
    width = TILE // cols
    start = tile_ref[0] * TILE
    root_row = start // (SITE_DEV * cols)
    blocks = TILE // BLOCK
    lane = lax.broadcasted_iota(jnp.int32, (8, BLOCK), 1)
    sub = lax.broadcasted_iota(jnp.int32, (8, BLOCK), 0)

    raw = [buf_ref[q * TILE_ROWS : (q + 1) * TILE_ROWS, :] for q in range(3)]
    fields, loc_x, loc_y = smooth(raw, root_row, table_ref, rows_mesh, grid_y)
    quant = quantities(fields, loc_x, loc_y, total_x)
    nugget = nugget_share * jnp.exp(2.0 * fields[3])
    for q in range(QUANT):
        rowq[q, :, :] = quant[q]
    rowq[QUANT, :, :] = nugget
    for g in range(TILE_ROWS):
        stack = jnp.concatenate(
            [quant[q][g : g + 1, :] for q in range(QUANT)] + [jnp.zeros((2, LANES), jnp.float32)],
            axis=0,
        )
        turned = jnp.transpose(stack)
        for q in range(QUANT):
            colq[q, g * LANES : (g + 1) * LANES, :] = jnp.broadcast_to(
                turned[:, q : q + 1], (LANES, LANES)
            )

    for k in range(cols):
        member = jnp.bitwise_xor(col, k)
        raw = [raws[k][q * SITE_ROWS : (q + 1) * SITE_ROWS, :] for q in range(3)]
        fields, loc_x, loc_y = smooth(raw, row, table_ref, rows_mesh, grid_y)
        if k == 0:
            for f in range(FIELDS):
                for j in range(SITE_ROWS):
                    fields_ref[f : f + 1, j * LANES : (j + 1) * LANES] = fields[f][j : j + 1, :]
        quant = quantities(fields, loc_x, loc_y, total_x)
        for q in range(QUANT):
            siteq[q, pl.ds(pl.multiple_of(member * SITE_ROWS, 8), SITE_ROWS), :] = quant[q]

    for j in range(blocks):
        lines = [jnp.broadcast_to(rowq[q, j : j + 1, :], (16, LANES)) for q in range(QUANT)]

        def tile_step(t, carry, j=j, lines=lines):
            base = pl.multiple_of(t * 16, 16)
            pick = [colq[q, pl.ds(base, 16), :] for q in range(QUANT)]
            gram[pl.ds(base, 16), at(j)] = covariance(pick, lines)
            return carry

        lax.fori_loop(j * BLOCK // 16, TILE // 16, tile_step, 0)

    for k in range(blocks):
        diagonal = []
        for i in range(BLOCK // 8):
            values = gram[k * BLOCK + 8 * i : k * BLOCK + 8 * i + 8, at(k)]
            nug = jnp.broadcast_to(rowq[QUANT, k : k + 1, :], (8, BLOCK))
            diagonal.append(values + jnp.where(lane - 8 * i == sub, nug, 0.0))
        own = inverse_factor(diagonal)
        inv[at(k), at(k)] = own
        if k > 0:
            inv[at(k), : k * BLOCK] = dot(own, inv[at(k), : k * BLOCK])
        if k + 1 < blocks:
            rest = slice((k + 1) * BLOCK, TILE)
            lower = dot_t(gram[rest, at(k)], own)
            for i in range(k + 1, blocks):
                mine = lower[(i - k - 1) * BLOCK : (i - k) * BLOCK, :]
                upto = slice((k + 1) * BLOCK, (i + 1) * BLOCK)
                gram[at(i), upto] = gram[at(i), upto] - dot_t(mine, lower[: (i - k) * BLOCK, :])
            if k > 0:
                inv[rest, : k * BLOCK] = inv[rest, : k * BLOCK] - dot(
                    lower, inv[at(k), : k * BLOCK]
                )
            inv[rest, at(k)] = -dot(lower, own)

    first = pl.multiple_of(col * width, width)
    depth = (col + 1) * (width // BLOCK)
    chunks = cols * SITE_DEV // CHUNK
    parts = CHUNK // LANES
    eye = lax.broadcasted_iota(jnp.int32, (BLOCK, LANES), 0) == lax.broadcasted_iota(
        jnp.int32, (BLOCK, LANES), 1
    )

    def chunk_step(ch, carry):
        lines = [
            [
                jnp.broadcast_to(siteq[q, pl.ds(ch * parts + p, 1), :], (8, LANES))
                for q in range(QUANT)
            ]
            for p in range(parts)
        ]
        here = pl.multiple_of(ch * CHUNK, CHUNK)

        def depth_step(kb, carry):
            base = pl.multiple_of(kb * BLOCK, BLOCK)
            for t in range(BLOCK // 8):
                pick = [colq[q, pl.ds(base + 8 * t, 8), :] for q in range(QUANT)]
                for p in range(parts):
                    cov[8 * t : 8 * t + 8, p * LANES : (p + 1) * LANES] = covariance(
                        pick, lines[p]
                    )
            for p in range(parts):
                same = start + base == row * (cols * SITE_DEV) + here + p * LANES

                @pl.when(same)
                def _(p=p):
                    nug = jnp.broadcast_to(rowq[QUANT, pl.ds(kb, 1), :], (BLOCK, LANES))
                    part = slice(p * LANES, (p + 1) * LANES)
                    cov[:, part] = cov[:, part] + jnp.where(eye, nug, 0.0)

            product = dot(inv[pl.ds(first, width), pl.ds(base, BLOCK)], cov[...])

            @pl.when(kb == 0)
            def _():
                solved[:, pl.ds(here, CHUNK)] = product

            @pl.when(kb > 0)
            def _():
                solved[:, pl.ds(here, CHUNK)] = solved[:, pl.ds(here, CHUNK)] + product

            return carry

        lax.fori_loop(0, depth, depth_step, 0)
        pltpu.make_async_copy(
            solved.at[:, pl.ds(here, CHUNK)], panel_ref.at[:, pl.ds(here, CHUNK)], sems.at[ch]
        ).start()
        return carry

    lax.fori_loop(0, chunks, chunk_step, 0)

    def finish(ch, carry):
        here = pl.multiple_of(ch * CHUNK, CHUNK)
        pltpu.make_async_copy(
            solved.at[:, pl.ds(here, CHUNK)], panel_ref.at[:, pl.ds(here, CHUNK)], sems.at[ch]
        ).wait()
        return carry

    lax.fori_loop(0, chunks, finish, 0)


def body(offsets, site_cell, estimates, panel_tile):
    rows_mesh = lax.axis_size("row")
    cols = lax.axis_size("col")
    devices = rows_mesh * cols
    assert FIELDS * CELL_X * CELL_Y * cols == LANES
    assert devices & (devices - 1) == 0
    vmem = pl.BlockSpec(memory_space=pltpu.VMEM)
    smem = pl.BlockSpec(memory_space=pltpu.SMEM)
    raw, buf = pl.pallas_call(
        functools.partial(pack_kernel, cols),
        out_shape=(
            jax.ShapeDtypeStruct((3 * SITE_ROWS, LANES), jnp.float32),
            jax.ShapeDtypeStruct((HEAD + rows_mesh, LANES), jnp.float32),
        ),
        in_specs=[smem, smem, vmem, vmem],
        out_specs=(vmem, vmem),
    )(panel_tile, estimates, offsets, site_cell.reshape(1, -1))
    raws = [raw]
    for k in range(1, cols):
        raws.append(lax.ppermute(raw, "col", [(i, i ^ k) for i in range(cols)]))
    step = 1
    while step < devices:
        pairs = [(i, i ^ step) for i in range(devices)]
        buf = buf + lax.ppermute(buf, ("row", "col"), pairs)
        step *= 2
    width = TILE // cols
    sites = cols * SITE_DEV
    panel, fields = pl.pallas_call(
        functools.partial(main_kernel, rows_mesh, cols),
        out_shape=(
            jax.ShapeDtypeStruct((width, sites), jnp.float32),
            jax.ShapeDtypeStruct((FIELDS, SITE_DEV), jnp.float32),
        ),
        in_specs=[smem, smem, vmem] + [vmem] * cols,
        out_specs=(pl.BlockSpec(memory_space=pl.ANY), vmem),
        scratch_shapes=[
            pltpu.VMEM((QUANT, TILE, LANES), jnp.float32),
            pltpu.VMEM((QUANT + 1, TILE_ROWS, LANES), jnp.float32),
            pltpu.VMEM((QUANT, cols * SITE_ROWS, LANES), jnp.float32),
            pltpu.VMEM((TILE, TILE), jnp.float32),
            pltpu.VMEM((TILE, TILE), jnp.float32),
            pltpu.VMEM((width, sites), jnp.float32),
            pltpu.VMEM((BLOCK, CHUNK), jnp.float32),
            pltpu.SemaphoreType.DMA((sites // CHUNK,)),
        ],
        compiler_params=pltpu.CompilerParams(vmem_limit_bytes=40 * 1024 * 1024),
    )(panel_tile, buf, buf, *raws)
    return (panel, fields)


def solution(mesh):
    placed = (P(None, ("row", "col")), P(("row", "col")), P(None, "row", "col"), P())
    return jax.shard_map(
        body,
        mesh=mesh,
        in_specs=placed,
        out_specs=(P("col", "row"), P(None, ("row", "col"))),
        check_vma=False,
    )
```

```python
import functools

import jax
import jax.numpy as jnp
from jax import lax
from jax.experimental import pallas as pl
from jax.experimental.pallas import tpu as pltpu
from jax.sharding import PartitionSpec as P

SITE_DEV = 1024
TILE = 512
CELL_X = 4
CELL_Y = 4
RADIUS = 2

spread_cells = 1.5
nugget_share = 0.5
range_shift = -0.7

LANES = 128
BLOCK = 128
FIELDS = 4
SITE_ROWS = SITE_DEV // LANES
TILE_ROWS = TILE // LANES
HEAD = 3 * TILE_ROWS
CHUNK = 256
QUANT = 6

HIGHEST = lax.Precision.HIGHEST


def dot(a, b):
    return jnp.dot(a, b, precision=HIGHEST, preferred_element_type=jnp.float32)


def dot_t(a, b):
    return lax.dot_general(
        a, b, (((1,), (1,)), ((), ())), precision=HIGHEST, preferred_element_type=jnp.float32
    )


def pack_kernel(cols, tile_ref, est_ref, offsets_ref, cell_ref, raw_ref, buf_ref):
    row = lax.axis_index("row")
    col = lax.axis_index("col")
    for j in range(SITE_ROWS):
        part = slice(j * LANES, (j + 1) * LANES)
        raw_ref[j : j + 1, :] = offsets_ref[0:1, part]
        raw_ref[SITE_ROWS + j : SITE_ROWS + j + 1, :] = offsets_ref[1:2, part]
        raw_ref[2 * SITE_ROWS + j : 2 * SITE_ROWS + j + 1, :] = cell_ref[0:1, part].astype(
            jnp.float32
        )
    start = tile_ref[0] * TILE
    root = start // SITE_DEV
    first = (start - root * SITE_DEV) // LANES
    mine = row * cols + col == root
    for q in range(3):
        rows = raw_ref[pl.ds(q * SITE_ROWS + first, TILE_ROWS), :]
        buf_ref[q * TILE_ROWS : (q + 1) * TILE_ROWS, :] = jnp.where(mine, rows, 0.0)
    grid_y = cols * CELL_Y
    lane = lax.broadcasted_iota(jnp.int32, (1, LANES), 1) - col * CELL_Y
    line = jnp.zeros((1, LANES), jnp.float32)
    for f in range(FIELDS):
        for a in range(CELL_X):
            for b in range(CELL_Y):
                line = jnp.where(
                    lane == (f * CELL_X + a) * grid_y + b, est_ref[f, a, b], line
                )
    count = buf_ref.shape[0] - HEAD
    index = lax.broadcasted_iota(jnp.int32, (count, LANES), 0)
    buf_ref[HEAD:, :] = jnp.where(index == row, jnp.broadcast_to(line, (count, LANES)), 0.0)


def smooth(raw, block_row, table_ref, rows_mesh, grid_y):
    off_x, off_y, cell = raw
    total_x = CELL_X * rows_mesh
    cell_x = jnp.floor((cell + 0.5) / grid_y)
    cell_y = cell - cell_x * grid_y
    loc_x = cell_x + off_x
    loc_y = cell_y + off_y
    weight_y = []
    for b in range(grid_y):
        dist = loc_y - (b + 0.5)
        value = jnp.exp(-dist * dist / (2.0 * spread_cells * spread_cells))
        weight_y.append(jnp.where(jnp.abs(cell_y - b) <= RADIUS, value, 0.0))
    sum_y = functools.reduce(jnp.add, weight_y)
    numer = [None] * FIELDS
    sum_x = None
    for a in range(CELL_X - RADIUS, 2 * CELL_X + RADIUS):
        coord = (block_row - 1) * CELL_X + a
        near = block_row - 1 + a // CELL_X
        line = HEAD + jnp.clip(near, 0, rows_mesh - 1)
        coord_f = coord.astype(jnp.float32)
        dist = loc_x - coord_f - 0.5
        value = jnp.exp(-dist * dist / (2.0 * spread_cells * spread_cells))
        inside = (coord >= 0) & (coord < total_x)
        reach = jnp.where(inside, float(RADIUS), -1.0)
        weight = jnp.where(jnp.abs(cell_x - coord_f) <= reach, value, 0.0)
        sum_x = weight if sum_x is None else sum_x + weight
        for f in range(FIELDS):
            base = (f * CELL_X + a % CELL_X) * grid_y
            inner = None
            for b in range(grid_y):
                term = table_ref[line, base + b] * weight_y[b]
                inner = term if inner is None else inner + term
            term = inner * weight
            numer[f] = term if numer[f] is None else numer[f] + term
    denom = sum_x * sum_y
    return [n / denom for n in numer], loc_x, loc_y


def quantities(fields, loc_x, loc_y, total_x):
    first = jnp.exp(2.0 * (fields[0] + range_shift))
    second = jnp.exp(2.0 * (fields[1] + range_shift))
    cosine = jnp.cos(fields[2])
    sine = jnp.sin(fields[2])
    half_a = 0.5 * (cosine * cosine * first + sine * sine * second)
    half_b = 0.5 * (sine * sine * first + cosine * cosine * second)
    half_c = 0.5 * (cosine * sine * (first - second))
    scale = jnp.exp(fields[3] + 0.5 * (fields[0] + fields[1] + 2.0 * range_shift))
    return [half_a, half_b, half_c, loc_x / total_x, loc_y / total_x, scale]


def covariance(cols, rows):
    m_aa = cols[0] + rows[0]
    m_bb = cols[1] + rows[1]
    m_ab = cols[2] + rows[2]
    diff_x = cols[3] - rows[3]
    diff_y = cols[4] - rows[4]
    inv_root = lax.rsqrt(m_aa * m_bb - m_ab * m_ab)
    form = diff_x * (m_bb * diff_x - m_ab * diff_y) + diff_y * (m_aa * diff_y - m_ab * diff_x)
    square = jnp.maximum(form * (3.0 * inv_root * inv_root), 1e-36)
    dist = square * lax.rsqrt(square)
    return (cols[5] * rows[5]) * inv_root * (1.0 + dist) * jnp.exp(-dist)


def lane_copy(values, lane):
    index = jnp.full(values.shape, lane, jnp.int32)
    return jnp.take_along_axis(values, index, axis=1)


def row_copy(values, row):
    return jnp.broadcast_to(values[row : row + 1, :], values.shape)


def inverse_factor(rows, beside):
    steps = BLOCK // 8
    lane = lax.broadcasted_iota(jnp.int32, (8, BLOCK), 1)
    sub = lax.broadcasted_iota(jnp.int32, (8, BLOCK), 0)
    rows = list(rows)
    out = [None] * steps
    for m in range(steps):
        at = 8 * m
        pivots = (lane >= at) & (lane < at + 8)
        column = [lane_copy(rows[m], at + c) for c in range(8)]
        block = jnp.where(lane - at == sub, 1.0, jnp.where(pivots, 0.0, rows[m]))
        solved = None
        inverse = None
        for c in range(8):
            pivot = row_copy(column[c], c)
            inv = 1.0 / pivot
            line = row_copy(block, c)
            scaled = line * lax.rsqrt(pivot)
            solved = scaled if c == 0 else jnp.where(sub == c, scaled, solved)
            inverse = inv if c == 0 else jnp.where(sub == c, inv, inverse)
            others = jnp.where(sub == c, 0.0, column[c])
            for j in range(c + 1, 8):
                column[j] = column[j] - (others * row_copy(column[j], c)) * inv
            block = block - (others * line) * inv
        out[m] = solved
        beside(m)
        if m == steps - 1:
            break
        block = block * inverse
        lines = [row_copy(block, c) for c in range(8)]
        for i in range(m + 1, steps):
            p = [lane_copy(rows[i], at + c) * lines[c] for c in range(8)]
            total = ((p[0] + p[1]) + (p[2] + p[3])) + ((p[4] + p[5]) + (p[6] + p[7]))
            rows[i] = jnp.where(pivots, 0.0, rows[i]) - total
    result = jnp.concatenate(out, axis=0)
    r = lax.broadcasted_iota(jnp.int32, (BLOCK, BLOCK), 0)
    c = lax.broadcasted_iota(jnp.int32, (BLOCK, BLOCK), 1)
    return jnp.where(c <= r, result, 0.0)


def at(block):
    return slice(block * BLOCK, (block + 1) * BLOCK)


def main_kernel(rows_mesh, cols, tile_ref, table_ref, buf_ref, *refs):
    raws = refs[:cols]
    panel_ref, fields_ref, colq, rowq, siteq, gram, lower, residual, solved, sems = refs[cols:]
    row = lax.axis_index("row")
    col = lax.axis_index("col")
    grid_y = cols * CELL_Y
    total_x = float(CELL_X * rows_mesh)
    width = TILE // cols
    start = tile_ref[0] * TILE
    root_row = start // (SITE_DEV * cols)
    blocks = TILE // BLOCK
    sites = cols * SITE_DEV
    chunks = sites // CHUNK
    parts = CHUNK // LANES
    lane = lax.broadcasted_iota(jnp.int32, (8, BLOCK), 1)
    sub = lax.broadcasted_iota(jnp.int32, (8, BLOCK), 0)

    raw = [buf_ref[q * TILE_ROWS : (q + 1) * TILE_ROWS, :] for q in range(3)]
    fields, loc_x, loc_y = smooth(raw, root_row, table_ref, rows_mesh, grid_y)
    quant = quantities(fields, loc_x, loc_y, total_x)
    nugget = nugget_share * jnp.exp(2.0 * fields[3])
    for q in range(QUANT):
        rowq[q, :, :] = quant[q]
    rowq[QUANT, :, :] = nugget
    for g in range(TILE_ROWS):
        stack = jnp.concatenate(
            [quant[q][g : g + 1, :] for q in range(QUANT)] + [jnp.zeros((2, LANES), jnp.float32)],
            axis=0,
        )
        turned = jnp.transpose(stack)
        for q in range(QUANT):
            colq[q, g * LANES : (g + 1) * LANES, :] = jnp.broadcast_to(
                turned[:, q : q + 1], (LANES, LANES)
            )

    for k in range(cols):
        member = jnp.bitwise_xor(col, k)
        raw = [raws[k][q * SITE_ROWS : (q + 1) * SITE_ROWS, :] for q in range(3)]
        fields, loc_x, loc_y = smooth(raw, row, table_ref, rows_mesh, grid_y)
        if k == 0:
            for f in range(FIELDS):
                for j in range(SITE_ROWS):
                    fields_ref[f : f + 1, j * LANES : (j + 1) * LANES] = fields[f][j : j + 1, :]
        quant = quantities(fields, loc_x, loc_y, total_x)
        for q in range(QUANT):
            siteq[q, pl.ds(pl.multiple_of(member * SITE_ROWS, 8), SITE_ROWS), :] = quant[q]

    for j in range(blocks):
        lines = [jnp.broadcast_to(rowq[q, j : j + 1, :], (16, LANES)) for q in range(QUANT)]

        def tile_step(t, carry, j=j, lines=lines):
            base = pl.multiple_of(t * 16, 16)
            pick = [colq[q, pl.ds(base, 16), :] for q in range(QUANT)]
            gram[pl.ds(base, 16), at(j)] = covariance(pick, lines)
            return carry

        lax.fori_loop(j * BLOCK // 16, TILE // 16, tile_step, 0)

    def copy_out(b, part):
        there = slice(b * BLOCK % width, b * BLOCK % width + BLOCK)
        return pltpu.make_async_copy(
            solved.at[at(b), part], panel_ref.at[there, part], sems.at[b]
        )

    own = None
    for k in range(blocks):
        diagonal = []
        for i in range(BLOCK // 8):
            values = gram[k * BLOCK + 8 * i : k * BLOCK + 8 * i + 8, at(k)]
            nug = jnp.broadcast_to(rowq[QUANT, k : k + 1, :], (8, BLOCK))
            diagonal.append(values + jnp.where(lane - 8 * i == sub, nug, 0.0))

        def panel_chunk(ch, k=k, own=own):
            part = slice(ch * CHUNK, (ch + 1) * CHUNK)
            past = None
            if k > 0:
                solved[at(k - 1), part] = dot(own, residual[:, part])
                past = dot(lower[at(k), : k * BLOCK], solved[: k * BLOCK, part])
            for p in range(parts):
                line = ch * parts + p
                lines = [
                    jnp.broadcast_to(siteq[q, line : line + 1, :], (8, LANES))
                    for q in range(QUANT)
                ]
                for t in range(BLOCK // 8):
                    rows = slice(k * BLOCK + 8 * t, k * BLOCK + 8 * t + 8)
                    value = covariance([colq[q, rows, :] for q in range(QUANT)], lines)
                    if past is not None:
                        value = value - past[8 * t : 8 * t + 8, p * LANES : (p + 1) * LANES]
                    residual[8 * t : 8 * t + 8, line * LANES : (line + 1) * LANES] = value

        def beside(m, panel_chunk=panel_chunk):
            steps = BLOCK // 8
            for ch in range(chunks):
                if ch * steps // chunks == m:
                    panel_chunk(ch)

        own = inverse_factor(diagonal, beside)
        if k > 0:

            @pl.when(col == (k - 1) * BLOCK // width)
            def _(k=k):
                copy_out(k - 1, slice(None)).start()

        offset = start + k * BLOCK - row * sites

        @pl.when((offset >= 0) & (offset < sites))
        def _(k=k, offset=offset):
            for i in range(BLOCK // 8):
                nug = jnp.broadcast_to(rowq[QUANT, k : k + 1, :], (8, LANES))
                here = pl.ds(pl.multiple_of(offset, LANES), LANES)
                rows = slice(8 * i, 8 * i + 8)
                residual[rows, here] = residual[rows, here] + jnp.where(
                    lane - 8 * i == sub, nug, 0.0
                )

        if k + 1 < blocks:
            rest = slice((k + 1) * BLOCK, TILE)
            part = dot_t(gram[rest, at(k)], own)
            lower[rest, at(k)] = part
            for i in range(k + 1, blocks):
                mine = part[(i - k - 1) * BLOCK : (i - k) * BLOCK, :]
                upto = slice((k + 1) * BLOCK, (i + 1) * BLOCK)
                gram[at(i), upto] = gram[at(i), upto] - dot_t(mine, part[: (i - k) * BLOCK, :])

    last = blocks - 1
    mine = col == last * BLOCK // width
    for ch in range(chunks):
        part = slice(ch * CHUNK, (ch + 1) * CHUNK)
        solved[at(last), part] = dot(own, residual[:, part])

        @pl.when(mine)
        def _(part=part):
            copy_out(last, part).start()

    for b in range(blocks):

        @pl.when(col == b * BLOCK // width)
        def _(b=b):
            copy_out(b, slice(None)).wait()


def body(offsets, site_cell, estimates, panel_tile):
    rows_mesh = lax.axis_size("row")
    cols = lax.axis_size("col")
    devices = rows_mesh * cols
    assert FIELDS * CELL_X * CELL_Y * cols == LANES
    assert devices & (devices - 1) == 0
    vmem = pl.BlockSpec(memory_space=pltpu.VMEM)
    smem = pl.BlockSpec(memory_space=pltpu.SMEM)
    raw, buf = pl.pallas_call(
        functools.partial(pack_kernel, cols),
        out_shape=(
            jax.ShapeDtypeStruct((3 * SITE_ROWS, LANES), jnp.float32),
            jax.ShapeDtypeStruct((HEAD + rows_mesh, LANES), jnp.float32),
        ),
        in_specs=[smem, smem, vmem, vmem],
        out_specs=(vmem, vmem),
    )(panel_tile, estimates, offsets, site_cell.reshape(1, -1))
    raws = [raw]
    for k in range(1, cols):
        raws.append(lax.ppermute(raw, "col", [(i, i ^ k) for i in range(cols)]))
    step = 1
    while step < devices:
        pairs = [(i, i ^ step) for i in range(devices)]
        buf = buf + lax.ppermute(buf, ("row", "col"), pairs)
        step *= 2
    width = TILE // cols
    sites = cols * SITE_DEV
    panel, fields = pl.pallas_call(
        functools.partial(main_kernel, rows_mesh, cols),
        out_shape=(
            jax.ShapeDtypeStruct((width, sites), jnp.float32),
            jax.ShapeDtypeStruct((FIELDS, SITE_DEV), jnp.float32),
        ),
        in_specs=[smem, smem, vmem] + [vmem] * cols,
        out_specs=(pl.BlockSpec(memory_space=pl.ANY), vmem),
        scratch_shapes=[
            pltpu.VMEM((QUANT, TILE, LANES), jnp.float32),
            pltpu.VMEM((QUANT + 1, TILE_ROWS, LANES), jnp.float32),
            pltpu.VMEM((QUANT, cols * SITE_ROWS, LANES), jnp.float32),
            pltpu.VMEM((TILE, TILE), jnp.float32),
            pltpu.VMEM((TILE, TILE), jnp.float32),
            pltpu.VMEM((BLOCK, sites), jnp.float32),
            pltpu.VMEM((TILE, sites), jnp.float32),
            pltpu.SemaphoreType.DMA((TILE // BLOCK,)),
        ],
        compiler_params=pltpu.CompilerParams(vmem_limit_bytes=40 * 1024 * 1024),
    )(panel_tile, buf, buf, *raws)
    return (panel, fields)


def solution(mesh):
    placed = (P(None, ("row", "col")), P(("row", "col")), P(None, "row", "col"), P())
    return jax.shard_map(
        body,
        mesh=mesh,
        in_specs=placed,
        out_specs=(P("col", "row"), P(None, ("row", "col"))),
        check_vma=False,
    )
```

```python
import functools

import jax
import jax.numpy as jnp
from jax import lax
from jax.experimental import pallas as pl
from jax.experimental.pallas import tpu as pltpu
from jax.sharding import PartitionSpec as P

SITE_DEV = 1024
TILE = 512
CELL_X = 4
CELL_Y = 4
RADIUS = 2

spread_cells = 1.5
nugget_share = 0.5
range_shift = -0.7

LANES = 128
BLOCK = 128
FIELDS = 4
SITE_ROWS = SITE_DEV // LANES
TILE_ROWS = TILE // LANES
RAW = 3 * SITE_ROWS
HEAD = 3 * TILE_ROWS
CHUNK = 256
QUANT = 5

HIGHEST = lax.Precision.HIGHEST


def dot(a, b):
    return jnp.dot(a, b, precision=HIGHEST, preferred_element_type=jnp.float32)


def dot_t(a, b):
    return lax.dot_general(
        a, b, (((1,), (1,)), ((), ())), precision=HIGHEST, preferred_element_type=jnp.float32
    )


def pack_kernel(cols, tile_ref, est_ref, offsets_ref, cell_ref, out_ref):
    row = lax.axis_index("row")
    col = lax.axis_index("col")
    for j in range(SITE_ROWS):
        part = slice(j * LANES, (j + 1) * LANES)
        out_ref[j : j + 1, :] = offsets_ref[0:1, part]
        out_ref[SITE_ROWS + j : SITE_ROWS + j + 1, :] = offsets_ref[1:2, part]
        out_ref[2 * SITE_ROWS + j : 2 * SITE_ROWS + j + 1, :] = cell_ref[0:1, part].astype(
            jnp.float32
        )
    start = tile_ref[0] * TILE
    root = start // SITE_DEV
    first = (start - root * SITE_DEV) // LANES
    mine = row * cols + col == root
    for q in range(3):
        rows = out_ref[pl.ds(q * SITE_ROWS + first, TILE_ROWS), :]
        there = RAW + q * TILE_ROWS
        out_ref[there : there + TILE_ROWS, :] = jnp.where(mine, rows, 0.0)
    grid_y = cols * CELL_Y
    lane = lax.broadcasted_iota(jnp.int32, (1, LANES), 1) - col * CELL_Y
    terms = []
    for f in range(FIELDS):
        for a in range(CELL_X):
            line = jnp.zeros((1, LANES), jnp.float32)
            for b in range(CELL_Y):
                line = jnp.where(
                    lane == (f * CELL_X + a) * grid_y + b, est_ref[f, a, b], line
                )
            terms.append(line)
    while len(terms) > 1:
        terms = [x + y for x, y in zip(terms[::2], terms[1::2])]
    count = out_ref.shape[0] - RAW - HEAD
    index = lax.broadcasted_iota(jnp.int32, (count, LANES), 0)
    out_ref[RAW + HEAD :, :] = jnp.where(
        index == row, jnp.broadcast_to(terms[0], (count, LANES)), 0.0
    )


def smooth(raw, block_row, table_ref, rows_mesh, grid_y):
    off_x, off_y, cell = raw
    total_x = CELL_X * rows_mesh
    cell_x = jnp.floor((cell + 0.5) / grid_y)
    cell_y = cell - cell_x * grid_y
    loc_x = cell_x + off_x
    loc_y = cell_y + off_y
    weight_y = []
    for b in range(grid_y):
        dist = loc_y - (b + 0.5)
        value = jnp.exp(-dist * dist / (2.0 * spread_cells * spread_cells))
        weight_y.append(jnp.where(jnp.abs(cell_y - b) <= RADIUS, value, 0.0))
    sum_y = functools.reduce(jnp.add, weight_y)
    numer = [None] * FIELDS
    sum_x = None
    for a in range(CELL_X - RADIUS, 2 * CELL_X + RADIUS):
        coord = (block_row - 1) * CELL_X + a
        near = block_row - 1 + a // CELL_X
        line = HEAD + jnp.clip(near, 0, rows_mesh - 1)
        coord_f = coord.astype(jnp.float32)
        dist = loc_x - coord_f - 0.5
        value = jnp.exp(-dist * dist / (2.0 * spread_cells * spread_cells))
        inside = (coord >= 0) & (coord < total_x)
        reach = jnp.where(inside, float(RADIUS), -1.0)
        weight = jnp.where(jnp.abs(cell_x - coord_f) <= reach, value, 0.0)
        sum_x = weight if sum_x is None else sum_x + weight
        for f in range(FIELDS):
            base = (f * CELL_X + a % CELL_X) * grid_y
            inner = None
            for b in range(grid_y):
                term = table_ref[line, base + b] * weight_y[b]
                inner = term if inner is None else inner + term
            term = inner * weight
            numer[f] = term if numer[f] is None else numer[f] + term
    denom = sum_x * sum_y
    return [n / denom for n in numer], loc_x, loc_y


def quantities(fields, loc_x, loc_y, total_x):
    first = jnp.exp(2.0 * (fields[0] + range_shift))
    second = jnp.exp(2.0 * (fields[1] + range_shift))
    cosine = jnp.cos(fields[2])
    sine = jnp.sin(fields[2])
    m_a = (cosine * cosine * first + sine * sine * second) * (1.0 / 6.0)
    m_b = (sine * sine * first + cosine * cosine * second) * (1.0 / 6.0)
    m_c = (cosine * sine * (first - second)) * (1.0 / 6.0)
    return [m_a, m_b, m_c, loc_x / total_x, loc_y / total_x]


def log_root(fields):
    return fields[0] + fields[1] + 2.0 * range_shift


def site_scale(fields):
    return jnp.exp(fields[3] + 0.5 * log_root(fields)) * (3.0**-0.5)


def scaled_nugget(fields):
    return (3.0 * nugget_share) * jnp.exp(-log_root(fields))


def covariance(cols, rows, scale=None):
    m_aa = cols[0] + rows[0]
    m_bb = cols[1] + rows[1]
    m_ab = cols[2] + rows[2]
    diff_x = cols[3] - rows[3]
    diff_y = cols[4] - rows[4]
    inv_root = lax.rsqrt(m_aa * m_bb - m_ab * m_ab)
    form = diff_x * (m_bb * diff_x - m_ab * diff_y) + diff_y * (m_aa * diff_y - m_ab * diff_x)
    form = jnp.maximum(form, 1e-36)
    dist = form * lax.rsqrt(form) * inv_root
    value = (inv_root + inv_root * dist) * jnp.exp(-dist)
    return value if scale is None else value * scale


def halves(values):
    high = values.astype(jnp.bfloat16)
    return high, (values - high.astype(jnp.float32)).astype(jnp.bfloat16)


def left_parts(values):
    high, low = halves(values)
    return jnp.concatenate([high, high, low], axis=1)


def right_parts(values):
    high, low = halves(values)
    return jnp.concatenate([high, low, high], axis=0)


def dot_parts(left, right):
    return jnp.dot(left, right, preferred_element_type=jnp.float32)


def lane_copy(values, lane):
    index = jnp.full(values.shape, lane, jnp.int32)
    return jnp.take_along_axis(values, index, axis=1)


def row_copy(values, row):
    return jnp.broadcast_to(values[row : row + 1, :], values.shape)


def inverse_factor(rows, beside):
    steps = BLOCK // 8
    lane = lax.broadcasted_iota(jnp.int32, (8, BLOCK), 1)
    sub = lax.broadcasted_iota(jnp.int32, (8, BLOCK), 0)
    rows = list(rows)
    out = [None] * steps
    for m in range(steps):
        at = 8 * m
        pivots = (lane >= at) & (lane < at + 8)
        column = [lane_copy(rows[m], at + c) for c in range(8)]
        block = jnp.where(lane - at == sub, 1.0, jnp.where(pivots, 0.0, rows[m]))
        solved = jnp.zeros((8, BLOCK), jnp.float32)
        pairs = []
        for c in range(0, 8, 2):
            p = row_copy(column[c], c)
            r = row_copy(column[c + 1], c)
            q = row_copy(column[c + 1], c + 1)
            det = p * q - r * r
            inv = 1.0 / det
            both = (sub == c) | (sub == c + 1)
            first = jnp.where(both, 0.0, column[c])
            second = jnp.where(both, 0.0, column[c + 1])
            left = q * first - r * second
            right = p * second - r * first
            upper = row_copy(block, c)
            under = row_copy(block, c + 1)
            solved = jnp.where(sub == c, upper * lax.rsqrt(p), solved)
            solved = jnp.where(
                sub == c + 1, (p * under - r * upper) * lax.rsqrt(p * det), solved
            )
            pairs.append((p, r, q, inv))
            if c + 2 < 8:
                left_inv = left * inv
                right_inv = right * inv
                for j in range(c + 2, 8):
                    a = row_copy(column[j], c)
                    b = row_copy(column[j], c + 1)
                    if j < c + 4:
                        column[j] = column[j] - (left * a + right * b) * inv
                    else:
                        column[j] = (column[j] - left_inv * a) - right_inv * b
                block = (block - left_inv * upper) - right_inv * under
            else:
                block = block - (left * upper + right * under) * inv
        out[m] = solved
        beside(m)
        if m == steps - 1:
            break
        lines = []
        for h, (p, r, q, inv) in enumerate(pairs):
            upper = row_copy(block, 2 * h)
            under = row_copy(block, 2 * h + 1)
            lines.append((q * upper - r * under) * inv)
            lines.append((p * under - r * upper) * inv)
        term = [lane_copy(rows[m + 1], at + c) * lines[c] for c in range(8)]
        total = [None] * steps
        total[m + 1] = ((term[0] + term[1]) + (term[2] + term[3])) + (
            (term[4] + term[5]) + (term[6] + term[7])
        )
        for c in range(8):
            for i in range(m + 2, steps):
                term = lane_copy(rows[i], at + c) * lines[c]
                total[i] = term if c == 0 else total[i] + term
        for i in range(m + 1, steps):
            rows[i] = jnp.where(pivots, 0.0, rows[i]) - total[i]
    result = jnp.concatenate(out, axis=0)
    r = lax.broadcasted_iota(jnp.int32, (BLOCK, BLOCK), 0)
    c = lax.broadcasted_iota(jnp.int32, (BLOCK, BLOCK), 1)
    return jnp.where(c <= r, result, 0.0)


def at(block):
    return slice(block * BLOCK, (block + 1) * BLOCK)


def main_kernel(rows_mesh, cols, tile_ref, table_ref, buf_ref, *refs):
    packs = refs[:cols]
    (
        panel_ref,
        fields_ref,
        raws,
        colq,
        rowq,
        siteq,
        gram,
        lower,
        left,
        right,
        residual,
        solved,
        raw_sems,
        sems,
    ) = refs[cols:]
    row = lax.axis_index("row")
    col = lax.axis_index("col")
    grid_y = cols * CELL_Y
    total_x = float(CELL_X * rows_mesh)
    width = TILE // cols
    start = tile_ref[0] * TILE
    root_row = start // (SITE_DEV * cols)
    blocks = TILE // BLOCK
    sites = cols * SITE_DEV
    chunks = sites // CHUNK
    parts = CHUNK // LANES
    steps = BLOCK // 8
    lane = lax.broadcasted_iota(jnp.int32, (8, BLOCK), 1)
    sub = lax.broadcasted_iota(jnp.int32, (8, BLOCK), 0)

    def raw_copy(k):
        return pltpu.make_async_copy(packs[k].at[0:RAW], raws.at[k], raw_sems.at[k])

    for k in range(cols):
        raw_copy(k).start()

    raw = [buf_ref[q * TILE_ROWS : (q + 1) * TILE_ROWS, :] for q in range(3)]
    fields, loc_x, loc_y = smooth(raw, root_row, table_ref, rows_mesh, grid_y)
    quant = quantities(fields, loc_x, loc_y, total_x)
    for q in range(QUANT):
        rowq[q, :, :] = quant[q]
    rowq[QUANT, :, :] = scaled_nugget(fields)
    for k in range(cols):
        raw_copy(k).wait()

    def panel_columns(g):
        pad = jnp.zeros((8 - QUANT, LANES), jnp.float32)
        turned = jnp.transpose(
            jnp.concatenate([quant[q][g : g + 1, :] for q in range(QUANT)] + [pad], axis=0)
        )
        for q in range(QUANT):
            colq[q, g * LANES : (g + 1) * LANES, :] = jnp.broadcast_to(
                turned[:, q : q + 1], (LANES, LANES)
            )

    def panel_gram(i, j):
        lines = [jnp.broadcast_to(rowq[q, j : j + 1, :], (8, LANES)) for q in range(QUANT)]
        for t in range(steps):
            rows = slice(i * BLOCK + 8 * t, i * BLOCK + 8 * t + 8)
            gram[rows, at(j)] = covariance([colq[q, rows, :] for q in range(QUANT)], lines)

    def site_rows():
        raw = [
            jnp.concatenate(
                [raws[k, q * SITE_ROWS : (q + 1) * SITE_ROWS, :] for k in range(cols)], axis=0
            )
            for q in range(3)
        ]
        fields, loc_x, loc_y = smooth(raw, row, table_ref, rows_mesh, grid_y)
        for f in range(FIELDS):
            for j in range(SITE_ROWS):
                fields_ref[f : f + 1, j * LANES : (j + 1) * LANES] = fields[f][j : j + 1, :]
        values = quantities(fields, loc_x, loc_y, total_x) + [site_scale(fields)]
        for k in range(cols):
            member = pl.multiple_of(jnp.bitwise_xor(col, k) * SITE_ROWS, 8)
            for q in range(QUANT + 1):
                siteq[q, pl.ds(member, SITE_ROWS), :] = values[q][
                    k * SITE_ROWS : (k + 1) * SITE_ROWS, :
                ]

    def copy_out(b, part):
        there = slice(b * BLOCK % width, b * BLOCK % width + BLOCK)
        return pltpu.make_async_copy(
            solved.at[at(b), part], panel_ref.at[there, part], sems.at[b]
        )

    def wide(j):
        return slice(3 * j * BLOCK, 3 * (j + 1) * BLOCK)

    def solve_chunk(k, own_parts, part):
        values = dot_parts(own_parts, right_parts(residual[:, part]))
        solved[at(k), part] = values
        return values

    def panel_chunk(ch, k, own_parts):
        part = slice(ch * CHUNK, (ch + 1) * CHUNK)
        past = None
        if k > 0:
            values = solve_chunk(k - 1, own_parts, part)
            right[wide(k - 1), part] = right_parts(values)
            past = dot_parts(left[at(k), : 3 * k * BLOCK], right[: 3 * k * BLOCK, part])
        for p in range(parts):
            line = ch * parts + p
            lines = [
                jnp.broadcast_to(siteq[q, line : line + 1, :], (8, LANES))
                for q in range(QUANT + 1)
            ]
            for t in range(steps):
                rows = slice(k * BLOCK + 8 * t, k * BLOCK + 8 * t + 8)
                value = covariance(
                    [colq[q, rows, :] for q in range(QUANT)], lines[:QUANT], lines[QUANT]
                )
                if past is not None:
                    value = value - past[8 * t : 8 * t + 8, p * LANES : (p + 1) * LANES]
                residual[8 * t : 8 * t + 8, line * LANES : (line + 1) * LANES] = value

    def lower_block(i, k, own):
        values = dot_t(gram[at(i), at(k)], own)
        lower[at(i), at(k)] = values
        left[at(i), wide(k)] = left_parts(values)

    def update_block(i, j, k):
        gram[at(i), at(j)] = gram[at(i), at(j)] - dot_t(lower[at(i), at(k)], lower[at(j), at(k)])

    panel_columns(0)
    panel_gram(0, 0)
    own = None
    for k in range(blocks):
        diagonal = []
        for i in range(steps):
            values = gram[k * BLOCK + 8 * i : k * BLOCK + 8 * i + 8, at(k)]
            nug = jnp.broadcast_to(rowq[QUANT, k : k + 1, :], (8, BLOCK))
            diagonal.append(values + jnp.where(lane - 8 * i == sub, nug, 0.0))
        own_parts = None if own is None else left_parts(own)

        def beside(m, k=k, own=own, own_parts=own_parts):
            if m == 0 and k == 0:
                site_rows()
            if k == 0 and 0 < m < blocks:
                panel_columns(m)
                for j in range(m + 1):
                    panel_gram(m, j)
            if m == 0 and k > 0:
                for i in range(k + 1, blocks):
                    lower_block(i, k - 1, own)
                    for j in range(k, i + 1):
                        update_block(i, j, k - 1)
            for ch in range(chunks):
                if ch * steps // chunks == m:
                    panel_chunk(ch, k, own_parts)

        own = inverse_factor(diagonal, beside)
        if k + 1 < blocks:
            lower_block(k + 1, k, own)
            update_block(k + 1, k + 1, k)
        if k > 0:

            @pl.when(col == (k - 1) * BLOCK // width)
            def _(k=k):
                copy_out(k - 1, slice(None)).start()

        offset = start + k * BLOCK - row * sites

        @pl.when((offset >= 0) & (offset < sites))
        def _(k=k, offset=offset):
            line = offset // LANES
            nug = rowq[QUANT, k : k + 1, :] * siteq[QUANT, pl.ds(line, 1), :]
            here = pl.ds(pl.multiple_of(offset, LANES), LANES)
            for i in range(steps):
                rows = slice(8 * i, 8 * i + 8)
                residual[rows, here] = residual[rows, here] + jnp.where(
                    lane - 8 * i == sub, jnp.broadcast_to(nug, (8, LANES)), 0.0
                )

    last = blocks - 1
    mine = col == last * BLOCK // width
    own_parts = left_parts(own)
    for ch in range(chunks):
        part = slice(ch * CHUNK, (ch + 1) * CHUNK)
        solve_chunk(last, own_parts, part)

        @pl.when(mine)
        def _(part=part):
            copy_out(last, part).start()

    for b in range(blocks):

        @pl.when(col == b * BLOCK // width)
        def _(b=b):
            copy_out(b, slice(None)).wait()


def body(offsets, site_cell, estimates, panel_tile):
    rows_mesh = lax.axis_size("row")
    cols = lax.axis_size("col")
    devices = rows_mesh * cols
    assert FIELDS * CELL_X * CELL_Y * cols == LANES
    assert devices & (devices - 1) == 0
    vmem = pl.BlockSpec(memory_space=pltpu.VMEM)
    smem = pl.BlockSpec(memory_space=pltpu.SMEM)
    pack = pl.pallas_call(
        functools.partial(pack_kernel, cols),
        out_shape=jax.ShapeDtypeStruct((RAW + HEAD + rows_mesh, LANES), jnp.float32),
        in_specs=[smem, smem, vmem, vmem],
        out_specs=vmem,
    )(panel_tile, estimates, offsets, site_cell.reshape(1, -1))
    packs = [pack]
    buf = pack[RAW:]
    step = 1
    while step < devices:
        pairs = [(i, i ^ step) for i in range(devices)]
        if step < cols:
            sent = jnp.concatenate([pack[:RAW], buf], axis=0) if step > 1 else pack
            near = lax.ppermute(sent, ("row", "col"), pairs)
            packs.append(near)
            for k in range(1, step):
                far = lax.ppermute(packs[k], ("row", "col"), pairs)
                packs.append(far)
            buf = buf + near[RAW:]
        else:
            buf = buf + lax.ppermute(buf, ("row", "col"), pairs)
        step *= 2
    width = TILE // cols
    sites = cols * SITE_DEV
    anywhere = pl.BlockSpec(memory_space=pl.ANY)
    panel, fields = pl.pallas_call(
        functools.partial(main_kernel, rows_mesh, cols),
        out_shape=(
            jax.ShapeDtypeStruct((width, sites), jnp.float32),
            jax.ShapeDtypeStruct((FIELDS, SITE_DEV), jnp.float32),
        ),
        in_specs=[smem, smem, vmem] + [anywhere] * cols,
        out_specs=(anywhere, vmem),
        scratch_shapes=[
            pltpu.VMEM((cols, RAW, LANES), jnp.float32),
            pltpu.VMEM((QUANT, TILE, LANES), jnp.float32),
            pltpu.VMEM((QUANT + 1, TILE_ROWS, LANES), jnp.float32),
            pltpu.VMEM((QUANT + 1, cols * SITE_ROWS, LANES), jnp.float32),
            pltpu.VMEM((TILE, TILE), jnp.float32),
            pltpu.VMEM((TILE, TILE), jnp.float32),
            pltpu.VMEM((TILE, 3 * TILE), jnp.bfloat16),
            pltpu.VMEM((3 * (TILE - BLOCK), sites), jnp.bfloat16),
            pltpu.VMEM((BLOCK, sites), jnp.float32),
            pltpu.VMEM((TILE, sites), jnp.float32),
            pltpu.SemaphoreType.DMA((cols,)),
            pltpu.SemaphoreType.DMA((TILE // BLOCK,)),
        ],
        compiler_params=pltpu.CompilerParams(vmem_limit_bytes=40 * 1024 * 1024),
    )(panel_tile, buf, buf, *packs)
    return (panel, fields)


def solution(mesh):
    placed = (P(None, ("row", "col")), P(("row", "col")), P(None, "row", "col"), P())
    return jax.shard_map(
        body,
        mesh=mesh,
        in_specs=placed,
        out_specs=(P("col", "row"), P(None, ("row", "col"))),
        check_vma=False,
    )
```

```python
import functools

import jax
import jax.numpy as jnp
from jax import lax
from jax.experimental import pallas as pl
from jax.experimental.pallas import tpu as pltpu
from jax.sharding import PartitionSpec as P

SITE_DEV = 1024
TILE = 512
CELL_X = 4
CELL_Y = 4
RADIUS = 2

spread_cells = 1.5
nugget_share = 0.5
range_shift = -0.7

LANES = 128
BLOCK = 128
FIELDS = 4
SITE_ROWS = SITE_DEV // LANES
TILE_ROWS = TILE // LANES
RAW = 3 * SITE_ROWS
HEAD = 3 * TILE_ROWS
CHUNK = 256
STRETCH = 4
LANE_ROWS = 14
FEATURES = 16
COPIES = 8

HIGHEST = lax.Precision.HIGHEST


def dot(a, b):
    return jnp.dot(a, b, precision=HIGHEST, preferred_element_type=jnp.float32)


def dot_t(a, b):
    return lax.dot_general(
        a, b, (((1,), (1,)), ((), ())), precision=HIGHEST, preferred_element_type=jnp.float32
    )


def pack_kernel(cols, tile_ref, est_ref, offsets_ref, cell_ref, out_ref):
    row = lax.axis_index("row")
    col = lax.axis_index("col")
    for j in range(SITE_ROWS):
        part = slice(j * LANES, (j + 1) * LANES)
        out_ref[j : j + 1, :] = offsets_ref[0:1, part]
        out_ref[SITE_ROWS + j : SITE_ROWS + j + 1, :] = offsets_ref[1:2, part]
        out_ref[2 * SITE_ROWS + j : 2 * SITE_ROWS + j + 1, :] = cell_ref[0:1, part].astype(
            jnp.float32
        )
    start = tile_ref[0] * TILE
    root = start // SITE_DEV
    first = (start - root * SITE_DEV) // LANES
    mine = row * cols + col == root
    for q in range(3):
        rows = out_ref[pl.ds(q * SITE_ROWS + first, TILE_ROWS), :]
        there = RAW + q * TILE_ROWS
        out_ref[there : there + TILE_ROWS, :] = jnp.where(mine, rows, 0.0)
    grid_y = cols * CELL_Y
    lane = lax.broadcasted_iota(jnp.int32, (1, LANES), 1) - col * CELL_Y
    terms = []
    for f in range(FIELDS):
        for a in range(CELL_X):
            line = jnp.zeros((1, LANES), jnp.float32)
            for b in range(CELL_Y):
                line = jnp.where(
                    lane == (f * CELL_X + a) * grid_y + b, est_ref[f, a, b], line
                )
            terms.append(line)
    while len(terms) > 1:
        terms = [x + y for x, y in zip(terms[::2], terms[1::2])]
    count = out_ref.shape[0] - RAW - HEAD
    index = lax.broadcasted_iota(jnp.int32, (count, LANES), 0)
    out_ref[RAW + HEAD :, :] = jnp.where(
        index == row, jnp.broadcast_to(terms[0], (count, LANES)), 0.0
    )


def smooth_pieces(get_raw, block_row, table_ref, rows_mesh, grid_y, result):
    total_x = CELL_X * rows_mesh
    state = {"numer": [None] * FIELDS, "sum_x": None}

    def begin():
        off_x, off_y, cell = get_raw()
        cell_x = jnp.floor((cell + 0.5) / grid_y)
        cell_y = cell - cell_x * grid_y
        state.update(cell_x=cell_x, loc_x=cell_x + off_x, loc_y=cell_y + off_y)
        weight_y = []
        for b in range(grid_y):
            dist = state["loc_y"] - (b + 0.5)
            value = jnp.exp(-dist * dist / (2.0 * spread_cells * spread_cells))
            weight_y.append(jnp.where(jnp.abs(cell_y - b) <= RADIUS, value, 0.0))
        state.update(weight_y=weight_y, sum_y=functools.reduce(jnp.add, weight_y))

    def add_column(a):
        coord = (block_row - 1) * CELL_X + a
        near = block_row - 1 + a // CELL_X
        line = HEAD + jnp.clip(near, 0, rows_mesh - 1)
        coord_f = coord.astype(jnp.float32)
        dist = state["loc_x"] - coord_f - 0.5
        value = jnp.exp(-dist * dist / (2.0 * spread_cells * spread_cells))
        inside = (coord >= 0) & (coord < total_x)
        reach = jnp.where(inside, float(RADIUS), -1.0)
        weight = jnp.where(jnp.abs(state["cell_x"] - coord_f) <= reach, value, 0.0)
        state["sum_x"] = weight if state["sum_x"] is None else state["sum_x"] + weight
        for f in range(FIELDS):
            base = (f * CELL_X + a % CELL_X) * grid_y
            inner = None
            for b in range(grid_y):
                term = table_ref[line, base + b] * state["weight_y"][b]
                inner = term if inner is None else inner + term
            term = inner * weight
            numer = state["numer"]
            numer[f] = term if numer[f] is None else numer[f] + term

    def end():
        denom = state["sum_x"] * state["sum_y"]
        result["fields"] = [n / denom for n in state["numer"]]
        result["loc"] = (state["loc_x"], state["loc_y"])

    columns = range(CELL_X - RADIUS, 2 * CELL_X + RADIUS)
    return (
        [(100, begin)]
        + [(150, functools.partial(add_column, a)) for a in columns]
        + [(20, end)]
    )


def smooth(raw, *args):
    result = {}
    for _, piece in smooth_pieces(lambda: raw, *args, result):
        piece()
    return result["fields"], *result["loc"]


def quantities(fields, loc_x, loc_y, centre, total_x):
    first = jnp.exp(2.0 * (fields[0] + range_shift))
    second = jnp.exp(2.0 * (fields[1] + range_shift))
    cosine = jnp.cos(fields[2])
    sine = jnp.sin(fields[2])
    m_a = (cosine * cosine * first + sine * sine * second) * (1.0 / 6.0)
    m_b = (sine * sine * first + cosine * cosine * second) * (1.0 / 6.0)
    m_c = (cosine * sine * (first - second)) * (1.0 / 6.0)
    return m_a, m_b, m_c, (loc_x - centre[0]) / total_x, (loc_y - centre[1]) / total_x


def log_root(fields):
    return fields[0] + fields[1] + 2.0 * range_shift


def site_scale(fields):
    return jnp.exp(fields[3] + 0.5 * log_root(fields)) * (3.0**-0.5)


def scaled_nugget(fields):
    return (3.0 * nugget_share) * jnp.exp(-log_root(fields))


def rows_of(quant):
    a, b, c, x, y = quant
    one = jnp.ones_like(a)
    own = b * x * x + a * y * y - 2.0 * c * x * y
    return [
        one,
        own,
        b,
        a,
        c,
        x * x,
        y * y,
        x * y,
        2.0 * (c * y - b * x),
        2.0 * (c * x - a * y),
        x,
        y,
        a * b - c * c,
    ]


def form_of(quant, weight):
    a, b, c, x, y = quant
    own = b * x * x + a * y * y - 2.0 * c * x * y
    values = [
        own,
        None,
        x * x,
        y * y,
        -2.0 * x * y,
        b,
        a,
        -2.0 * c,
        x,
        y,
        2.0 * (c * y - b * x),
        2.0 * (c * x - a * y),
    ]
    return [weight if v is None else v * weight for v in values]


def det_of(quant, weight):
    a, b, c, _, _ = quant
    values = [a * b - c * c, None, b, a, -2.0 * c]
    values = [v if v is None else v * weight for v in values]
    return {0: values[0], 2: values[3], 3: values[2], 4: values[4], 12: weight}


def thirds(values):
    high = values.astype(jnp.bfloat16)
    rest = values - high.astype(jnp.float32)
    low = rest.astype(jnp.bfloat16)
    return high, low, (rest - low.astype(jnp.float32)).astype(jnp.bfloat16)


LEFT_ORDER = (0, 0, 1, 1, 0, 2, 1, 2)
RIGHT_ORDER = (0, 1, 0, 1, 2, 0, 2, 1)


def covariance(det, form):
    inv_root = lax.rsqrt(det)
    form = jnp.maximum(form, 1e-36)
    dist = form * lax.rsqrt(form) * inv_root
    return (inv_root + inv_root * dist) * jnp.exp(-dist)


def halves(values):
    high = values.astype(jnp.bfloat16)
    return high, (values - high.astype(jnp.float32)).astype(jnp.bfloat16)


def left_parts(values):
    high, low = halves(values)
    return jnp.concatenate([high, high, low], axis=1)


def right_parts(values):
    high, low = halves(values)
    return jnp.concatenate([high, low, high], axis=0)


def dot_parts(left, right):
    return jnp.dot(left, right, preferred_element_type=jnp.float32)


def lane_copy(values, lane):
    index = jnp.full(values.shape, lane, jnp.int32)
    return jnp.take_along_axis(values, index, axis=1)


def row_copy(values, row):
    return jnp.broadcast_to(values[row : row + 1, :], values.shape)


def factor_step(m, work, lines_ref, own_ref):
    steps = BLOCK // 8
    lane = lax.broadcasted_iota(jnp.int32, (8, BLOCK), 1)
    sub = lax.broadcasted_iota(jnp.int32, (8, BLOCK), 0)
    at = 8 * m
    before = at - 8

    def row(i):
        return work[8 * i : 8 * i + 8, :]

    def set_row(i, values):
        work[8 * i : 8 * i + 8, :] = values

    def updated(values, first, lines):
        term = [lane_copy(values, first + c) * lines[c] for c in range(8)]
        total = ((term[0] + term[1]) + (term[2] + term[3])) + (
            (term[4] + term[5]) + (term[6] + term[7])
        )
        return jnp.where((lane >= first) & (lane < first + 8), 0.0, values) - total

    here = row(m)
    column = [lane_copy(here, at + c) for c in range(8)]
    if m > 0:
        if m + 1 < steps:
            past = [jnp.broadcast_to(lines_ref[c : c + 1, :], (8, BLOCK)) for c in range(8)]
            following = updated(row(m + 1), before, past)
        near = min(m + 2 + LANE_ROWS, steps)
        total = {}
        for c in range(8):
            for i in range(m + 2, near):
                term = lane_copy(row(i), before + c) * past[c]
                total[i] = term if c == 0 else total[i] + term
        for i in range(m + 2, near):
            gone = (lane >= before) & (lane < at)
            set_row(i, jnp.where(gone, 0.0, row(i)) - total[i])
        if near < steps:
            rest = work[8 * near :, :]
            gone = lax.broadcasted_iota(jnp.int32, rest.shape, 1)
            gone = (gone >= before) & (gone < at)
            work[8 * near :, :] = jnp.where(gone, 0.0, rest) - dot(
                rest[:, before:at], lines_ref[...]
            )
    elif m + 1 < steps:
        following = row(m + 1)
    pivots = (lane >= at) & (lane < at + 8)
    block = jnp.where(lane - at == sub, 1.0, jnp.where(pivots, 0.0, here))
    solved = jnp.zeros((8, BLOCK), jnp.float32)
    pairs = []
    for c in range(0, 8, 2):
        p = row_copy(column[c], c)
        r = row_copy(column[c + 1], c)
        q = row_copy(column[c + 1], c + 1)
        det = p * q - r * r
        inv = 1.0 / det
        both = (sub == c) | (sub == c + 1)
        first = jnp.where(both, 0.0, column[c])
        second = jnp.where(both, 0.0, column[c + 1])
        left = q * first - r * second
        right = p * second - r * first
        upper = row_copy(block, c)
        under = row_copy(block, c + 1)
        solved = jnp.where(sub == c, upper * lax.rsqrt(p), solved)
        solved = jnp.where(sub == c + 1, (p * under - r * upper) * lax.rsqrt(p * det), solved)
        pairs.append((p, r, q, inv))
        if c + 2 < 8:
            left_inv = left * inv
            right_inv = right * inv
            for j in range(c + 2, 8):
                a = row_copy(column[j], c)
                b = row_copy(column[j], c + 1)
                if j < c + 4:
                    column[j] = column[j] - (left * a + right * b) * inv
                else:
                    column[j] = (column[j] - left_inv * a) - right_inv * b
            block = (block - left_inv * upper) - right_inv * under
        else:
            block = block - (left * upper + right * under) * inv
    own_ref[at : at + 8, :] = jnp.where(lane <= at + sub, solved, 0.0)
    if m == steps - 1:
        return
    lines = []
    for h, (p, r, q, inv) in enumerate(pairs):
        upper = row_copy(block, 2 * h)
        under = row_copy(block, 2 * h + 1)
        lines.append((q * upper - r * under) * inv)
        lines.append((p * under - r * upper) * inv)
    set_row(m + 1, updated(following, at, lines))
    for c in range(8):
        lines_ref[c : c + 1, :] = lines[c][c : c + 1, :]


def at(block):
    return slice(block * BLOCK, (block + 1) * BLOCK)


def main_kernel(rows_mesh, cols, tile_ref, table_ref, buf_ref, *refs):
    packs = refs[:cols]
    (
        panel_ref,
        fields_ref,
        raws,
        nugget,
        scales,
        feats,
        panel_left,
        panel_det,
        panel_form,
        site_feats,
        site_det,
        site_form,
        gram,
        owns,
        lower,
        left,
        right,
        operand,
        work,
        lines_ref,
        residual,
        solved,
        raw_sems,
        sems,
    ) = refs[cols:]
    row = lax.axis_index("row")
    col = lax.axis_index("col")
    grid_y = cols * CELL_Y
    total_x = float(CELL_X * rows_mesh)
    width = TILE // cols
    start = tile_ref[0] * TILE
    root_row = start // (SITE_DEV * cols)
    blocks = TILE // BLOCK
    sites = cols * SITE_DEV
    chunks = sites // CHUNK
    site_lines = sites // LANES
    steps = BLOCK // 8
    lane = lax.broadcasted_iota(jnp.int32, (8, BLOCK), 1)
    sub = lax.broadcasted_iota(jnp.int32, (8, BLOCK), 0)
    centre = (
        (root_row * CELL_X).astype(jnp.float32) + 0.5 * CELL_X,
        0.5 * grid_y,
    )

    def raw_copy(k):
        return pltpu.make_async_copy(packs[k].at[0:RAW], raws.at[k], raw_sems.at[k])

    for k in range(cols):
        raw_copy(k).start()

    raw = [buf_ref[q * TILE_ROWS : (q + 1) * TILE_ROWS, :] for q in range(3)]
    fields, loc_x, loc_y = smooth(raw, root_row, table_ref, rows_mesh, grid_y)
    quant = quantities(fields, loc_x, loc_y, centre, total_x)
    nugget[...] = scaled_nugget(fields)
    one = jnp.ones_like(quant[0])
    feats[...] = jnp.zeros(feats.shape, jnp.float32)
    for n, values in enumerate((rows_of(quant), form_of(quant, one), det_of(quant, one))):
        values = values if isinstance(values, dict) else dict(enumerate(values))
        for f, value in values.items():
            for g in range(TILE_ROWS):
                feats[n, f : f + 1, g * LANES : (g + 1) * LANES] = value[g : g + 1, :]
    for k in range(cols):
        raw_copy(k).wait()

    def put_parts(target, values, lanes):
        parts = thirds(values)
        for n, part in enumerate(RIGHT_ORDER):
            target[n * FEATURES : (n + 1) * FEATURES, lanes] = parts[part]

    def panel_features(g):
        lanes = slice(g * LANES, (g + 1) * LANES)
        parts = [p.astype(jnp.float32) for p in thirds(feats[0, :, lanes])]
        stack = jnp.concatenate([parts[part] for part in LEFT_ORDER], axis=0)
        panel_left[lanes, :] = jnp.transpose(stack).astype(jnp.bfloat16)
        put_parts(panel_form, feats[1, :, lanes], lanes)
        put_parts(panel_det, feats[2, :, lanes], lanes)

    def panel_gram(i, j):
        gram[at(i), at(j)] = covariance(
            dot_parts(panel_left[at(i), :], panel_det[:, at(j)]),
            dot_parts(panel_left[at(i), :], panel_form[:, at(j)]),
        )

    def site_rows():
        raw = [
            jnp.concatenate(
                [raws[k, q * SITE_ROWS : (q + 1) * SITE_ROWS, :] for k in range(cols)], axis=0
            )
            for q in range(3)
        ]
        fields, loc_x, loc_y = smooth(raw, row, table_ref, rows_mesh, grid_y)
        for f in range(FIELDS):
            for j in range(SITE_ROWS):
                fields_ref[f : f + 1, j * LANES : (j + 1) * LANES] = fields[f][j : j + 1, :]
        quant = quantities(fields, loc_x, loc_y, centre, total_x)
        scale = site_scale(fields)
        inverse = 1.0 / scale
        weight = inverse * inverse
        site_feats[...] = jnp.zeros(site_feats.shape, jnp.float32)
        for k in range(cols):
            member = jnp.bitwise_xor(col, k) * SITE_ROWS
            mine = slice(k * SITE_ROWS, (k + 1) * SITE_ROWS)
            scales[pl.ds(pl.multiple_of(member, 8), SITE_ROWS), :] = scale[mine, :]
            for n, values in enumerate((form_of(quant, weight), det_of(quant, weight))):
                values = values if isinstance(values, dict) else dict(enumerate(values))
                for f, value in values.items():
                    for j in range(SITE_ROWS):
                        there = pl.multiple_of((member + j) * LANES, LANES)
                        at_row = k * SITE_ROWS + j
                        site_feats[n, f : f + 1, pl.ds(there, LANES)] = value[
                            at_row : at_row + 1, :
                        ]

    def site_parts(line):
        lanes = slice(line * LANES, (line + 1) * LANES)
        put_parts(site_form, site_feats[0, :, lanes], lanes)
        put_parts(site_det, site_feats[1, :, lanes], lanes)

    def copy_out(b, part):
        there = slice(b * BLOCK % width, b * BLOCK % width + BLOCK)
        return pltpu.make_async_copy(
            solved.at[at(b), part], panel_ref.at[there, part], sems.at[b]
        )

    def wide(j):
        return slice(3 * j * BLOCK, 3 * (j + 1) * BLOCK)

    def chunk_of(ch):
        return slice(ch * CHUNK, (ch + 1) * CHUNK)

    taken = set()
    fresh = set()

    def fresh_line(k, line):
        lanes = slice(line * LANES, (line + 1) * LANES)
        value = covariance(
            dot_parts(panel_left[at(k), :], site_det[:, lanes]),
            dot_parts(panel_left[at(k), :], site_form[:, lanes]),
        )
        fresh.add((k, line))
        if (k, line) in taken:
            value = value + residual[k % 2, :, lanes]
        residual[k % 2, :, lanes] = value

    def take_solved(k, ch):
        values = dot_parts(left[at(k), : 3 * k * BLOCK], right[: 3 * k * BLOCK, chunk_of(ch)])
        for p in range(CHUNK // LANES):
            line = ch * (CHUNK // LANES) + p
            lanes = slice(line * LANES, (line + 1) * LANES)
            part = values[:, p * LANES : (p + 1) * LANES]
            taken.add((k, line))
            residual[k % 2, :, lanes] = (
                residual[k % 2, :, lanes] - part if (k, line) in fresh else -part
            )

    def split_residual(k, ch):
        operand[ch % 2] = right_parts(residual[k % 2, :, chunk_of(ch)])

    def solve_chunk(k, ch):
        solved[at(k), chunk_of(ch)] = dot_parts(left[at(k), wide(k)], operand[ch % 2])

    def split_solved(k, ch):
        right[wide(k), chunk_of(ch)] = right_parts(solved[at(k), chunk_of(ch)])

    def lower_block(i, k):
        values = dot_t(gram[at(i), at(k)], owns[k])
        lower[at(i), at(k)] = values
        left[at(i), wide(k)] = left_parts(values)

    def update_block(i, j, k):
        gram[at(i), at(j)] = gram[at(i), at(j)] - dot_t(lower[at(i), at(k)], lower[at(j), at(k)])

    def stretch(code):
        pl.when(tile_ref[0] >= 0)(code)

    def shared(count, m):
        return [n for n in range(count) if n * steps // count == m]

    def beside(k, m):
        if k == 0:
            pairs = [(i, j) for i in range(1, blocks) for j in range(i + 1)]
            if m == 0:
                for g in range(1, TILE_ROWS):
                    panel_features(g)
            for n in shared(len(pairs), m - 1) if m > 0 else ():
                panel_gram(*pairs[n])
            for line in shared(site_lines, m):
                site_parts(line)
            for line in shared(site_lines, m - 1) if m > 0 else ():
                fresh_line(0, line)
            return
        others = [(i, j) for i in range(k + 1, blocks) for j in range(k, i + 1)]
        if 0 < m <= len(others):
            update_block(*others[m - 1], k - 1)
        for line in shared(site_lines, m):
            fresh_line(k, line)
        period = steps // chunks
        ch = m // period
        if m % period == 0:
            if m == 0:
                split_residual(k - 1, 0)
            solve_chunk(k - 1, ch)
        if m % period == period - 1:
            if ch + 1 < chunks:
                split_residual(k - 1, ch + 1)
            split_solved(k - 1, ch)
            if ch > 0:
                take_solved(k, ch - 1)

    def beside_update(k):
        if k == 0:
            for line in shared(site_lines, steps - 1):
                fresh_line(0, line)
            return
        take_solved(k, chunks - 1)

    site_rows()
    panel_features(0)
    panel_gram(0, 0)
    for k in range(blocks):

        for first in range(0, steps, STRETCH):

            @stretch
            def _(k=k, first=first):
                for i in range(steps) if first == 0 else ():
                    rows = slice(8 * i, 8 * i + 8)
                    values = gram[k * BLOCK + 8 * i : k * BLOCK + 8 * i + 8, at(k)]
                    nug = jnp.broadcast_to(nugget[k : k + 1, :], (8, BLOCK))
                    work[rows, :] = values + jnp.where(lane - 8 * i == sub, nug, 0.0)
                for m in range(first, first + STRETCH):
                    factor_step(m, work, lines_ref, owns.at[k])
                    beside(k, m)

        @stretch
        def _(k=k):
            if k + 1 < blocks:
                lower_block(k + 1, k)
                update_block(k + 1, k + 1, k)
            for i in range(k + 2, blocks):
                lower_block(i, k)
            left[at(k), wide(k)] = left_parts(owns[k])
            beside_update(k)

        if k > 0:

            @pl.when(col == (k - 1) * BLOCK // width)
            def _(k=k):
                copy_out(k - 1, slice(None)).start()

        offset = start + k * BLOCK - row * sites

        @pl.when((offset >= 0) & (offset < sites))
        def _(k=k, offset=offset):
            nug = nugget[k : k + 1, :] * scales[pl.ds(offset // LANES, 1), :]
            here = pl.ds(pl.multiple_of(offset, LANES), LANES)
            for i in range(steps):
                rows = slice(8 * i, 8 * i + 8)
                residual[k % 2, rows, here] = residual[k % 2, rows, here] + jnp.where(
                    lane - 8 * i == sub, jnp.broadcast_to(nug, (8, LANES)), 0.0
                )

    last = blocks - 1
    mine = col == last * BLOCK // width
    for ch in range(chunks):
        part = slice(ch * CHUNK, (ch + 1) * CHUNK)
        split_residual(last, ch)
        solve_chunk(last, ch)

        @pl.when(mine)
        def _(part=part):
            copy_out(last, part).start()

    for b in range(blocks):

        @pl.when(col == b * BLOCK // width)
        def _(b=b):
            copy_out(b, slice(None)).wait()


def body(offsets, site_cell, estimates, panel_tile):
    rows_mesh = lax.axis_size("row")
    cols = lax.axis_size("col")
    devices = rows_mesh * cols
    assert FIELDS * CELL_X * CELL_Y * cols == LANES
    assert devices & (devices - 1) == 0
    vmem = pl.BlockSpec(memory_space=pltpu.VMEM)
    smem = pl.BlockSpec(memory_space=pltpu.SMEM)
    pack = pl.pallas_call(
        functools.partial(pack_kernel, cols),
        out_shape=jax.ShapeDtypeStruct((RAW + HEAD + rows_mesh, LANES), jnp.float32),
        in_specs=[smem, smem, vmem, vmem],
        out_specs=vmem,
    )(panel_tile, estimates, offsets, site_cell.reshape(1, -1))
    packs = [pack]
    buf = pack[RAW:]
    step = 1
    while step < devices:
        pairs = [(i, i ^ step) for i in range(devices)]
        if step < cols:
            sent = jnp.concatenate([pack[:RAW], buf], axis=0) if step > 1 else pack
            near = lax.ppermute(sent, ("row", "col"), pairs)
            packs.append(near)
            for k in range(1, step):
                far = lax.ppermute(packs[k], ("row", "col"), pairs)
                packs.append(far)
            buf = buf + near[RAW:]
        else:
            buf = buf + lax.ppermute(buf, ("row", "col"), pairs)
        step *= 2
    width = TILE // cols
    sites = cols * SITE_DEV
    anywhere = pl.BlockSpec(memory_space=pl.ANY)
    panel, fields = pl.pallas_call(
        functools.partial(main_kernel, rows_mesh, cols),
        out_shape=(
            jax.ShapeDtypeStruct((width, sites), jnp.float32),
            jax.ShapeDtypeStruct((FIELDS, SITE_DEV), jnp.float32),
        ),
        in_specs=[smem, smem, vmem] + [anywhere] * cols,
        out_specs=(anywhere, vmem),
        scratch_shapes=[
            pltpu.VMEM((cols, RAW, LANES), jnp.float32),
            pltpu.VMEM((TILE_ROWS, LANES), jnp.float32),
            pltpu.VMEM((cols * SITE_ROWS, LANES), jnp.float32),
            pltpu.VMEM((3, FEATURES, TILE), jnp.float32),
            pltpu.VMEM((TILE, COPIES * FEATURES), jnp.bfloat16),
            pltpu.VMEM((COPIES * FEATURES, TILE), jnp.bfloat16),
            pltpu.VMEM((COPIES * FEATURES, TILE), jnp.bfloat16),
            pltpu.VMEM((2, FEATURES, sites), jnp.float32),
            pltpu.VMEM((COPIES * FEATURES, sites), jnp.bfloat16),
            pltpu.VMEM((COPIES * FEATURES, sites), jnp.bfloat16),
            pltpu.VMEM((TILE, TILE), jnp.float32),
            pltpu.VMEM((TILE // BLOCK, BLOCK, BLOCK), jnp.float32),
            pltpu.VMEM((TILE, TILE), jnp.float32),
            pltpu.VMEM((TILE, 3 * TILE), jnp.bfloat16),
            pltpu.VMEM((3 * (TILE - BLOCK), sites), jnp.bfloat16),
            pltpu.VMEM((2, 3 * BLOCK, CHUNK), jnp.bfloat16),
            pltpu.VMEM((BLOCK, BLOCK), jnp.float32),
            pltpu.VMEM((8, BLOCK), jnp.float32),
            pltpu.VMEM((2, BLOCK, sites), jnp.float32),
            pltpu.VMEM((TILE, sites), jnp.float32),
            pltpu.SemaphoreType.DMA((cols,)),
            pltpu.SemaphoreType.DMA((TILE // BLOCK,)),
        ],
        compiler_params=pltpu.CompilerParams(vmem_limit_bytes=40 * 1024 * 1024),
    )(panel_tile, buf, buf, *packs)
    return (panel, fields)


def solution(mesh):
    placed = (P(None, ("row", "col")), P(("row", "col")), P(None, "row", "col"), P())
    return jax.shard_map(
        body,
        mesh=mesh,
        in_specs=placed,
        out_specs=(P("col", "row"), P(None, ("row", "col"))),
        check_vma=False,
    )
```

```python
import functools

import jax
import jax.numpy as jnp
from jax import lax
from jax.experimental import pallas as pl
from jax.experimental.pallas import tpu as pltpu
from jax.sharding import PartitionSpec as P

SITE_DEV = 1024
TILE = 512
CELL_X = 4
CELL_Y = 4
RADIUS = 2

spread_cells = 1.5
nugget_share = 0.5
range_shift = -0.7

LANES = 128
BLOCK = 128
FIELDS = 4
SITE_ROWS = SITE_DEV // LANES
TILE_ROWS = TILE // LANES
RAW = 3 * SITE_ROWS
HEAD = 3 * TILE_ROWS
CHUNK = 256
STRETCH = 4
FEATURES = 16
COPIES = 8

HIGHEST = lax.Precision.HIGHEST


def dot(a, b):
    return jnp.dot(a, b, precision=HIGHEST, preferred_element_type=jnp.float32)


def dot_t(a, b):
    return lax.dot_general(
        a, b, (((1,), (1,)), ((), ())), precision=HIGHEST, preferred_element_type=jnp.float32
    )


def pack_kernel(cols, tile_ref, est_ref, offsets_ref, cell_ref, out_ref):
    row = lax.axis_index("row")
    col = lax.axis_index("col")
    for j in range(SITE_ROWS):
        part = slice(j * LANES, (j + 1) * LANES)
        out_ref[j : j + 1, :] = offsets_ref[0:1, part]
        out_ref[SITE_ROWS + j : SITE_ROWS + j + 1, :] = offsets_ref[1:2, part]
        out_ref[2 * SITE_ROWS + j : 2 * SITE_ROWS + j + 1, :] = cell_ref[0:1, part].astype(
            jnp.float32
        )
    start = tile_ref[...][0, 0] * TILE
    root = start // SITE_DEV
    first = (start - root * SITE_DEV) // LANES
    mine = row * cols + col == root
    for q in range(3):
        rows = out_ref[pl.ds(q * SITE_ROWS + first, TILE_ROWS), :]
        there = RAW + q * TILE_ROWS
        out_ref[there : there + TILE_ROWS, :] = jnp.where(mine, rows, 0.0)
    grid_y = cols * CELL_Y
    lane = lax.broadcasted_iota(jnp.int32, (1, LANES), 1) - col * CELL_Y
    terms = []
    for f in range(FIELDS):
        for a in range(CELL_X):
            line = jnp.zeros((1, LANES), jnp.float32)
            for b in range(CELL_Y):
                line = jnp.where(
                    lane == (f * CELL_X + a) * grid_y + b, est_ref[f, a, b], line
                )
            terms.append(line)
    while len(terms) > 1:
        terms = [x + y for x, y in zip(terms[::2], terms[1::2])]
    count = out_ref.shape[0] - RAW - HEAD
    index = lax.broadcasted_iota(jnp.int32, (count, LANES), 0)
    out_ref[RAW + HEAD :, :] = jnp.where(
        index == row, jnp.broadcast_to(terms[0], (count, LANES)), 0.0
    )


def smooth_pieces(get_raw, block_row, table_ref, rows_mesh, grid_y, result):
    total_x = CELL_X * rows_mesh
    state = {"numer": [None] * FIELDS, "sum_x": None}

    def begin():
        off_x, off_y, cell = get_raw()
        cell_x = jnp.floor((cell + 0.5) / grid_y)
        cell_y = cell - cell_x * grid_y
        state.update(cell_x=cell_x, loc_x=cell_x + off_x, loc_y=cell_y + off_y)
        weight_y = []
        for b in range(grid_y):
            dist = state["loc_y"] - (b + 0.5)
            value = jnp.exp(-dist * dist / (2.0 * spread_cells * spread_cells))
            weight_y.append(jnp.where(jnp.abs(cell_y - b) <= RADIUS, value, 0.0))
        state.update(weight_y=weight_y, sum_y=functools.reduce(jnp.add, weight_y))

    def add_column(a):
        coord = (block_row - 1) * CELL_X + a
        near = block_row - 1 + a // CELL_X
        line = HEAD + jnp.clip(near, 0, rows_mesh - 1)
        coord_f = coord.astype(jnp.float32)
        dist = state["loc_x"] - coord_f - 0.5
        value = jnp.exp(-dist * dist / (2.0 * spread_cells * spread_cells))
        inside = (coord >= 0) & (coord < total_x)
        reach = jnp.where(inside, float(RADIUS), -1.0)
        weight = jnp.where(jnp.abs(state["cell_x"] - coord_f) <= reach, value, 0.0)
        state["sum_x"] = weight if state["sum_x"] is None else state["sum_x"] + weight
        for f in range(FIELDS):
            base = (f * CELL_X + a % CELL_X) * grid_y
            inner = None
            for b in range(grid_y):
                term = table_ref[line, base + b] * state["weight_y"][b]
                inner = term if inner is None else inner + term
            term = inner * weight
            numer = state["numer"]
            numer[f] = term if numer[f] is None else numer[f] + term

    def end():
        denom = state["sum_x"] * state["sum_y"]
        result["fields"] = [n / denom for n in state["numer"]]
        result["loc"] = (state["loc_x"], state["loc_y"])

    columns = range(CELL_X - RADIUS, 2 * CELL_X + RADIUS)
    return (
        [(100, begin)]
        + [(150, functools.partial(add_column, a)) for a in columns]
        + [(20, end)]
    )


def smooth(raw, *args):
    result = {}
    for _, piece in smooth_pieces(lambda: raw, *args, result):
        piece()
    return result["fields"], *result["loc"]


def quantities(fields, loc_x, loc_y, centre, total_x):
    first = jnp.exp(2.0 * (fields[0] + range_shift))
    second = jnp.exp(2.0 * (fields[1] + range_shift))
    cosine = jnp.cos(fields[2])
    sine = jnp.sin(fields[2])
    m_a = (cosine * cosine * first + sine * sine * second) * (1.0 / 6.0)
    m_b = (sine * sine * first + cosine * cosine * second) * (1.0 / 6.0)
    m_c = (cosine * sine * (first - second)) * (1.0 / 6.0)
    return m_a, m_b, m_c, (loc_x - centre[0]) / total_x, (loc_y - centre[1]) / total_x


def log_root(fields):
    return fields[0] + fields[1] + 2.0 * range_shift


def site_scale(fields):
    return jnp.exp(fields[3] + 0.5 * log_root(fields)) * (3.0**-0.5)


def scaled_nugget(fields):
    return (3.0 * nugget_share) * jnp.exp(-log_root(fields))


def rows_of(quant):
    a, b, c, x, y = quant
    one = jnp.ones_like(a)
    own = b * x * x + a * y * y - 2.0 * c * x * y
    return [
        one,
        own,
        b,
        a,
        c,
        x * x,
        y * y,
        x * y,
        2.0 * (c * y - b * x),
        2.0 * (c * x - a * y),
        x,
        y,
        a * b - c * c,
    ]


def form_of(quant, weight):
    a, b, c, x, y = quant
    own = b * x * x + a * y * y - 2.0 * c * x * y
    values = [
        own,
        None,
        x * x,
        y * y,
        -2.0 * x * y,
        b,
        a,
        -2.0 * c,
        x,
        y,
        2.0 * (c * y - b * x),
        2.0 * (c * x - a * y),
    ]
    return [weight if v is None else v * weight for v in values]


def det_of(quant, weight):
    a, b, c, _, _ = quant
    values = [a * b - c * c, None, b, a, -2.0 * c]
    values = [v if v is None else v * weight for v in values]
    return {0: values[0], 2: values[3], 3: values[2], 4: values[4], 12: weight}


def thirds(values):
    high = values.astype(jnp.bfloat16)
    rest = values - high.astype(jnp.float32)
    low = rest.astype(jnp.bfloat16)
    return high, low, (rest - low.astype(jnp.float32)).astype(jnp.bfloat16)


LEFT_ORDER = (0, 0, 1, 1, 0, 2, 1, 2)
RIGHT_ORDER = (0, 1, 0, 1, 2, 0, 2, 1)


def covariance(det, form):
    inv_root = lax.rsqrt(det)
    form = jnp.maximum(form, 1e-36)
    dist = form * lax.rsqrt(form) * inv_root
    return (inv_root + inv_root * dist) * jnp.exp(-dist)


def halves(values):
    high = values.astype(jnp.bfloat16)
    return high, (values - high.astype(jnp.float32)).astype(jnp.bfloat16)


def left_parts(values):
    high, low = halves(values)
    return jnp.concatenate([high, high, low], axis=1)


def right_parts(values):
    high, low = halves(values)
    return jnp.concatenate([high, low, high], axis=0)


def dot_parts(left, right):
    return jnp.dot(left, right, preferred_element_type=jnp.float32)


def lane_copy(values, lane):
    index = jnp.full(values.shape, lane, jnp.int32)
    return jnp.take_along_axis(values, index, axis=1)


def row_copy(values, row):
    return jnp.broadcast_to(values[row : row + 1, :], values.shape)


def factor_step(m, work, lines_ref, own_ref):
    steps = BLOCK // 8
    lane = lax.broadcasted_iota(jnp.int32, (8, BLOCK), 1)
    sub = lax.broadcasted_iota(jnp.int32, (8, BLOCK), 0)
    at = 8 * m
    before = at - 8

    def row(i):
        return work[8 * i : 8 * i + 8, :]

    def set_row(i, values):
        work[8 * i : 8 * i + 8, :] = values

    def updated(values, first, lines):
        term = [lane_copy(values, first + c) * lines[c] for c in range(8)]
        total = ((term[0] + term[1]) + (term[2] + term[3])) + (
            (term[4] + term[5]) + (term[6] + term[7])
        )
        return jnp.where((lane >= first) & (lane < first + 8), 0.0, values) - total

    here = row(m)
    column = [lane_copy(here, at + c) for c in range(8)]
    if m > 0:
        if m + 1 < steps:
            past = [jnp.broadcast_to(lines_ref[c : c + 1, :], (8, BLOCK)) for c in range(8)]
            following = updated(row(m + 1), before, past)
        total = {}
        for c in range(8):
            for i in range(m + 2, steps):
                term = lane_copy(row(i), before + c) * past[c]
                total[i] = term if c == 0 else total[i] + term
        for i in range(m + 2, steps):
            gone = (lane >= before) & (lane < at)
            set_row(i, jnp.where(gone, 0.0, row(i)) - total[i])
    elif m + 1 < steps:
        following = row(m + 1)
    pivots = (lane >= at) & (lane < at + 8)
    block = jnp.where(lane - at == sub, 1.0, jnp.where(pivots, 0.0, here))
    solved = jnp.zeros((8, BLOCK), jnp.float32)
    pairs = []
    for c in range(0, 8, 2):
        p = row_copy(column[c], c)
        r = row_copy(column[c + 1], c)
        q = row_copy(column[c + 1], c + 1)
        det = p * q - r * r
        inv = 1.0 / det
        both = (sub == c) | (sub == c + 1)
        first = jnp.where(both, 0.0, column[c])
        second = jnp.where(both, 0.0, column[c + 1])
        left = q * first - r * second
        right = p * second - r * first
        upper = row_copy(block, c)
        under = row_copy(block, c + 1)
        solved = jnp.where(sub == c, upper * lax.rsqrt(p), solved)
        solved = jnp.where(sub == c + 1, (p * under - r * upper) * lax.rsqrt(p * det), solved)
        pairs.append((p, r, q, inv))
        if c + 2 < 8:
            left_inv = left * inv
            right_inv = right * inv
            for j in range(c + 2, 8):
                a = row_copy(column[j], c)
                b = row_copy(column[j], c + 1)
                if j < c + 4:
                    column[j] = column[j] - (left * a + right * b) * inv
                else:
                    column[j] = (column[j] - left_inv * a) - right_inv * b
            block = (block - left_inv * upper) - right_inv * under
        else:
            block = block - (left * upper + right * under) * inv
    own_ref[at : at + 8, :] = jnp.where(lane <= at + sub, solved, 0.0)
    if m == steps - 1:
        return
    lines = []
    for h, (p, r, q, inv) in enumerate(pairs):
        upper = row_copy(block, 2 * h)
        under = row_copy(block, 2 * h + 1)
        lines.append((q * upper - r * under) * inv)
        lines.append((p * under - r * upper) * inv)
    set_row(m + 1, updated(following, at, lines))
    for c in range(8):
        lines_ref[c : c + 1, :] = lines[c][c : c + 1, :]


def at(block):
    return slice(block * BLOCK, (block + 1) * BLOCK)


def main_kernel(rows_mesh, cols, tile_ref, table_ref, buf_ref, *refs):
    packs = refs[:cols]
    (
        panel_ref,
        fields_ref,
        raws,
        nugget,
        scales,
        feats,
        panel_left,
        panel_det,
        panel_form,
        site_feats,
        site_det,
        site_form,
        gram,
        owns,
        lower,
        left,
        right,
        operand,
        work,
        lines_ref,
        residual,
        solved,
        raw_sems,
        sems,
    ) = refs[cols:]
    row = lax.axis_index("row")
    col = lax.axis_index("col")
    grid_y = cols * CELL_Y
    total_x = float(CELL_X * rows_mesh)
    width = TILE // cols
    tile = tile_ref[...][0, 0]
    start = tile * TILE
    root_row = start // (SITE_DEV * cols)
    blocks = TILE // BLOCK
    sites = cols * SITE_DEV
    chunks = sites // CHUNK
    site_lines = sites // LANES
    steps = BLOCK // 8
    lane = lax.broadcasted_iota(jnp.int32, (8, BLOCK), 1)
    sub = lax.broadcasted_iota(jnp.int32, (8, BLOCK), 0)
    centre = (
        (root_row * CELL_X).astype(jnp.float32) + 0.5 * CELL_X,
        0.5 * grid_y,
    )

    def raw_copy(k):
        return pltpu.make_async_copy(packs[k].at[0:RAW], raws.at[k], raw_sems.at[k])

    for k in range(cols):
        raw_copy(k).start()

    raw = [buf_ref[q * TILE_ROWS : (q + 1) * TILE_ROWS, :] for q in range(3)]
    fields, loc_x, loc_y = smooth(raw, root_row, table_ref, rows_mesh, grid_y)
    quant = quantities(fields, loc_x, loc_y, centre, total_x)
    nugget[...] = scaled_nugget(fields)
    one = jnp.ones_like(quant[0])
    feats[...] = jnp.zeros(feats.shape, jnp.float32)
    for n, values in enumerate((rows_of(quant), form_of(quant, one), det_of(quant, one))):
        values = values if isinstance(values, dict) else dict(enumerate(values))
        for f, value in values.items():
            for g in range(TILE_ROWS):
                feats[n, f : f + 1, g * LANES : (g + 1) * LANES] = value[g : g + 1, :]
    for k in range(cols):
        raw_copy(k).wait()

    def put_parts(target, values, lanes):
        parts = thirds(values)
        for n, part in enumerate(RIGHT_ORDER):
            target[n * FEATURES : (n + 1) * FEATURES, lanes] = parts[part]

    def panel_features(g):
        lanes = slice(g * LANES, (g + 1) * LANES)
        parts = [p.astype(jnp.float32) for p in thirds(feats[0, :, lanes])]
        stack = jnp.concatenate([parts[part] for part in LEFT_ORDER], axis=0)
        panel_left[lanes, :] = jnp.transpose(stack).astype(jnp.bfloat16)
        put_parts(panel_form, feats[1, :, lanes], lanes)
        put_parts(panel_det, feats[2, :, lanes], lanes)

    def panel_gram(i, j):
        gram[at(i), at(j)] = covariance(
            dot_parts(panel_left[at(i), :], panel_det[:, at(j)]),
            dot_parts(panel_left[at(i), :], panel_form[:, at(j)]),
        )

    def site_rows():
        raw = [
            jnp.concatenate(
                [raws[k, q * SITE_ROWS : (q + 1) * SITE_ROWS, :] for k in range(cols)], axis=0
            )
            for q in range(3)
        ]
        fields, loc_x, loc_y = smooth(raw, row, table_ref, rows_mesh, grid_y)
        for f in range(FIELDS):
            for j in range(SITE_ROWS):
                fields_ref[f : f + 1, j * LANES : (j + 1) * LANES] = fields[f][j : j + 1, :]
        quant = quantities(fields, loc_x, loc_y, centre, total_x)
        scale = site_scale(fields)
        inverse = 1.0 / scale
        weight = inverse * inverse
        site_feats[...] = jnp.zeros(site_feats.shape, jnp.float32)
        for k in range(cols):
            member = jnp.bitwise_xor(col, k) * SITE_ROWS
            mine = slice(k * SITE_ROWS, (k + 1) * SITE_ROWS)
            scales[pl.ds(pl.multiple_of(member, 8), SITE_ROWS), :] = scale[mine, :]
            for n, values in enumerate((form_of(quant, weight), det_of(quant, weight))):
                values = values if isinstance(values, dict) else dict(enumerate(values))
                for f, value in values.items():
                    for j in range(SITE_ROWS):
                        there = pl.multiple_of((member + j) * LANES, LANES)
                        at_row = k * SITE_ROWS + j
                        site_feats[n, f : f + 1, pl.ds(there, LANES)] = value[
                            at_row : at_row + 1, :
                        ]

    def site_parts(line):
        lanes = slice(line * LANES, (line + 1) * LANES)
        put_parts(site_form, site_feats[0, :, lanes], lanes)
        put_parts(site_det, site_feats[1, :, lanes], lanes)

    def copy_out(b, part):
        there = slice(b * BLOCK % width, b * BLOCK % width + BLOCK)
        return pltpu.make_async_copy(
            solved.at[at(b), part], panel_ref.at[there, part], sems.at[b]
        )

    def wide(j):
        return slice(3 * j * BLOCK, 3 * (j + 1) * BLOCK)

    def chunk_of(ch):
        return slice(ch * CHUNK, (ch + 1) * CHUNK)

    taken = set()
    fresh = set()

    def fresh_line(k, line):
        lanes = slice(line * LANES, (line + 1) * LANES)
        value = covariance(
            dot_parts(panel_left[at(k), :], site_det[:, lanes]),
            dot_parts(panel_left[at(k), :], site_form[:, lanes]),
        )
        fresh.add((k, line))
        if (k, line) in taken:
            value = value + residual[k % 2, :, lanes]
        residual[k % 2, :, lanes] = value

    def take_solved(k, ch):
        values = dot_parts(left[at(k), : 3 * k * BLOCK], right[: 3 * k * BLOCK, chunk_of(ch)])
        for p in range(CHUNK // LANES):
            line = ch * (CHUNK // LANES) + p
            lanes = slice(line * LANES, (line + 1) * LANES)
            part = values[:, p * LANES : (p + 1) * LANES]
            taken.add((k, line))
            residual[k % 2, :, lanes] = (
                residual[k % 2, :, lanes] - part if (k, line) in fresh else -part
            )

    def split_residual(k, ch):
        operand[ch % 2] = right_parts(residual[k % 2, :, chunk_of(ch)])

    def solve_chunk(k, ch):
        solved[at(k), chunk_of(ch)] = dot_parts(left[at(k), wide(k)], operand[ch % 2])

    def split_solved(k, ch):
        right[wide(k), chunk_of(ch)] = right_parts(solved[at(k), chunk_of(ch)])

    def lower_block(i, k):
        values = dot_t(gram[at(i), at(k)], owns[k])
        lower[at(i), at(k)] = values
        left[at(i), wide(k)] = left_parts(values)

    def update_block(i, j, k):
        gram[at(i), at(j)] = gram[at(i), at(j)] - dot_t(lower[at(i), at(k)], lower[at(j), at(k)])

    bounds = iter(range(0, -1000, -1))

    def stretch(code):
        pl.when(tile >= next(bounds))(code)

    def shared(count, m):
        return [n for n in range(count) if n * steps // count == m]

    def beside(k, m):
        if k == 0:
            pairs = [(i, j) for i in range(1, blocks) for j in range(i + 1)]
            if m == 0:
                for g in range(1, TILE_ROWS):
                    panel_features(g)
            for n in shared(len(pairs), m - 1) if m > 0 else ():
                panel_gram(*pairs[n])
            for line in shared(site_lines, m):
                site_parts(line)
            for line in shared(site_lines, m - 1) if m > 0 else ():
                fresh_line(0, line)
            return
        others = [(i, j) for i in range(k + 1, blocks) for j in range(k, i + 1)]
        if 0 < m <= len(others):
            update_block(*others[m - 1], k - 1)
        for line in shared(site_lines, m):
            fresh_line(k, line)
        period = steps // chunks
        ch = m // period
        if m % period == 0:
            if m == 0:
                split_residual(k - 1, 0)
            solve_chunk(k - 1, ch)
        if m % period == period - 1:
            if ch + 1 < chunks:
                split_residual(k - 1, ch + 1)
            split_solved(k - 1, ch)
            if ch > 0:
                take_solved(k, ch - 1)

    def beside_update(k):
        if k == 0:
            for line in shared(site_lines, steps - 1):
                fresh_line(0, line)
            return
        take_solved(k, chunks - 1)

    site_rows()
    panel_features(0)
    panel_gram(0, 0)
    for k in range(blocks):

        for first in range(0, steps, STRETCH):

            @stretch
            def _(k=k, first=first):
                for i in range(steps) if first == 0 else ():
                    rows = slice(8 * i, 8 * i + 8)
                    values = gram[k * BLOCK + 8 * i : k * BLOCK + 8 * i + 8, at(k)]
                    nug = jnp.broadcast_to(nugget[k : k + 1, :], (8, BLOCK))
                    work[rows, :] = values + jnp.where(lane - 8 * i == sub, nug, 0.0)
                for m in range(first, first + STRETCH):
                    factor_step(m, work, lines_ref, owns.at[k])
                    beside(k, m)

        @stretch
        def _(k=k):
            if k + 1 < blocks:
                lower_block(k + 1, k)
                update_block(k + 1, k + 1, k)
            for i in range(k + 2, blocks):
                lower_block(i, k)
            left[at(k), wide(k)] = left_parts(owns[k])
            beside_update(k)

        if k > 0:

            @pl.when(col == (k - 1) * BLOCK // width)
            def _(k=k):
                copy_out(k - 1, slice(None)).start()

        offset = start + k * BLOCK - row * sites

        @pl.when((offset >= 0) & (offset < sites))
        def _(k=k, offset=offset):
            nug = nugget[k : k + 1, :] * scales[pl.ds(offset // LANES, 1), :]
            here = pl.ds(pl.multiple_of(offset, LANES), LANES)
            for i in range(steps):
                rows = slice(8 * i, 8 * i + 8)
                residual[k % 2, rows, here] = residual[k % 2, rows, here] + jnp.where(
                    lane - 8 * i == sub, jnp.broadcast_to(nug, (8, LANES)), 0.0
                )

    last = blocks - 1
    mine = col == last * BLOCK // width
    for ch in range(chunks):
        part = slice(ch * CHUNK, (ch + 1) * CHUNK)
        split_residual(last, ch)
        solve_chunk(last, ch)

        @pl.when(mine)
        def _(part=part):
            copy_out(last, part).start()

    for b in range(blocks):

        @pl.when(col == b * BLOCK // width)
        def _(b=b):
            copy_out(b, slice(None)).wait()


def body(offsets, site_cell, estimates, panel_tile):
    rows_mesh = lax.axis_size("row")
    cols = lax.axis_size("col")
    devices = rows_mesh * cols
    assert FIELDS * CELL_X * CELL_Y * cols == LANES
    assert devices & (devices - 1) == 0
    vmem = pl.BlockSpec(memory_space=pltpu.VMEM)
    smem = pl.BlockSpec(memory_space=pltpu.SMEM)
    pack = pl.pallas_call(
        functools.partial(pack_kernel, cols),
        out_shape=pltpu.VMEM((RAW + HEAD + rows_mesh, LANES), jnp.float32),
        in_specs=[vmem, smem, vmem, vmem],
        out_specs=vmem,
    )(panel_tile.reshape(1, 1), estimates, offsets, site_cell.reshape(1, -1))
    packs = [pack]
    buf = pack[RAW:]
    step = 1
    while step < devices:
        pairs = [(i, i ^ step) for i in range(devices)]
        if step < cols:
            sent = jnp.concatenate([pack[:RAW], buf], axis=0) if step > 1 else pack
            near = lax.ppermute(sent, ("row", "col"), pairs)
            packs.append(near)
            for k in range(1, step):
                far = lax.ppermute(packs[k], ("row", "col"), pairs)
                packs.append(far)
            buf = buf + near[RAW:]
        else:
            buf = buf + lax.ppermute(buf, ("row", "col"), pairs)
        step *= 2
    width = TILE // cols
    sites = cols * SITE_DEV
    anywhere = pl.BlockSpec(memory_space=pl.ANY)
    panel, fields = pl.pallas_call(
        functools.partial(main_kernel, rows_mesh, cols),
        out_shape=(
            jax.ShapeDtypeStruct((width, sites), jnp.float32),
            jax.ShapeDtypeStruct((FIELDS, SITE_DEV), jnp.float32),
        ),
        in_specs=[vmem, smem, vmem] + [anywhere] * cols,
        out_specs=(anywhere, vmem),
        scratch_shapes=[
            pltpu.VMEM((cols, RAW, LANES), jnp.float32),
            pltpu.VMEM((TILE_ROWS, LANES), jnp.float32),
            pltpu.VMEM((cols * SITE_ROWS, LANES), jnp.float32),
            pltpu.VMEM((3, FEATURES, TILE), jnp.float32),
            pltpu.VMEM((TILE, COPIES * FEATURES), jnp.bfloat16),
            pltpu.VMEM((COPIES * FEATURES, TILE), jnp.bfloat16),
            pltpu.VMEM((COPIES * FEATURES, TILE), jnp.bfloat16),
            pltpu.VMEM((2, FEATURES, sites), jnp.float32),
            pltpu.VMEM((COPIES * FEATURES, sites), jnp.bfloat16),
            pltpu.VMEM((COPIES * FEATURES, sites), jnp.bfloat16),
            pltpu.VMEM((TILE, TILE), jnp.float32),
            pltpu.VMEM((TILE // BLOCK, BLOCK, BLOCK), jnp.float32),
            pltpu.VMEM((TILE, TILE), jnp.float32),
            pltpu.VMEM((TILE, 3 * TILE), jnp.bfloat16),
            pltpu.VMEM((3 * (TILE - BLOCK), sites), jnp.bfloat16),
            pltpu.VMEM((2, 3 * BLOCK, CHUNK), jnp.bfloat16),
            pltpu.VMEM((BLOCK, BLOCK), jnp.float32),
            pltpu.VMEM((8, BLOCK), jnp.float32),
            pltpu.VMEM((2, BLOCK, sites), jnp.float32),
            pltpu.VMEM((TILE, sites), jnp.float32),
            pltpu.SemaphoreType.DMA((cols,)),
            pltpu.SemaphoreType.DMA((TILE // BLOCK,)),
        ],
        compiler_params=pltpu.CompilerParams(
            vmem_limit_bytes=40 * 1024 * 1024,
        ),
    )(panel_tile.reshape(1, 1), buf, buf, *packs)
    return (panel, fields)


def solution(mesh):
    placed = (P(None, ("row", "col")), P(("row", "col")), P(None, "row", "col"), P())
    return jax.shard_map(
        body,
        mesh=mesh,
        in_specs=placed,
        out_specs=(P("col", "row"), P(None, ("row", "col"))),
        check_vma=False,
    )
```

```python
import functools

import jax
import jax.numpy as jnp
from jax import lax
from jax.experimental import pallas as pl
from jax.experimental.pallas import tpu as pltpu
from jax.sharding import PartitionSpec as P

SITE_DEV = 1024
TILE = 512
CELL_X = 4
CELL_Y = 4
RADIUS = 2

spread_cells = 1.5
nugget_share = 0.5
range_shift = -0.7

LANES = 128
BLOCK = 128
FIELDS = 4
SITE_ROWS = SITE_DEV // LANES
TILE_ROWS = TILE // LANES
RAW = 3 * SITE_ROWS
HEAD = 3 * TILE_ROWS
CHUNK = 256
STRETCH = 4
FEATURES = 16
COPIES = 8

HIGHEST = lax.Precision.HIGHEST


def dot(a, b):
    return jnp.dot(a, b, precision=HIGHEST, preferred_element_type=jnp.float32)


def dot_t(a, b):
    return lax.dot_general(
        a, b, (((1,), (1,)), ((), ())), precision=HIGHEST, preferred_element_type=jnp.float32
    )


def pack_kernel(cols, tile_ref, est_ref, offsets_ref, cell_ref, out_ref):
    row = lax.axis_index("row")
    col = lax.axis_index("col")
    for j in range(SITE_ROWS):
        part = slice(j * LANES, (j + 1) * LANES)
        out_ref[j : j + 1, :] = offsets_ref[0:1, part]
        out_ref[SITE_ROWS + j : SITE_ROWS + j + 1, :] = offsets_ref[1:2, part]
        out_ref[2 * SITE_ROWS + j : 2 * SITE_ROWS + j + 1, :] = cell_ref[0:1, part].astype(
            jnp.float32
        )
    start = tile_ref[...][0, 0] * TILE
    root = start // SITE_DEV
    first = (start - root * SITE_DEV) // LANES
    mine = row * cols + col == root
    for q in range(3):
        rows = out_ref[pl.ds(q * SITE_ROWS + first, TILE_ROWS), :]
        there = RAW + q * TILE_ROWS
        out_ref[there : there + TILE_ROWS, :] = jnp.where(mine, rows, 0.0)
    grid_y = cols * CELL_Y
    lane = lax.broadcasted_iota(jnp.int32, (1, LANES), 1) - col * CELL_Y
    terms = []
    for f in range(FIELDS):
        for a in range(CELL_X):
            line = jnp.zeros((1, LANES), jnp.float32)
            for b in range(CELL_Y):
                line = jnp.where(
                    lane == (f * CELL_X + a) * grid_y + b, est_ref[f, a, b], line
                )
            terms.append(line)
    while len(terms) > 1:
        terms = [x + y for x, y in zip(terms[::2], terms[1::2])]
    count = out_ref.shape[0] - RAW - HEAD
    index = lax.broadcasted_iota(jnp.int32, (count, LANES), 0)
    out_ref[RAW + HEAD :, :] = jnp.where(
        index == row, jnp.broadcast_to(terms[0], (count, LANES)), 0.0
    )


def smooth_pieces(get_raw, block_row, table_ref, rows_mesh, grid_y, result):
    total_x = CELL_X * rows_mesh
    state = {"numer": [None] * FIELDS, "sum_x": None}

    def begin():
        off_x, off_y, cell = get_raw()
        cell_x = jnp.floor((cell + 0.5) / grid_y)
        cell_y = cell - cell_x * grid_y
        state.update(cell_x=cell_x, loc_x=cell_x + off_x, loc_y=cell_y + off_y)
        weight_y = []
        for b in range(grid_y):
            dist = state["loc_y"] - (b + 0.5)
            value = jnp.exp(-dist * dist / (2.0 * spread_cells * spread_cells))
            weight_y.append(jnp.where(jnp.abs(cell_y - b) <= RADIUS, value, 0.0))
        state.update(weight_y=weight_y, sum_y=functools.reduce(jnp.add, weight_y))

    def add_column(a):
        coord = (block_row - 1) * CELL_X + a
        near = block_row - 1 + a // CELL_X
        line = HEAD + jnp.clip(near, 0, rows_mesh - 1)
        coord_f = coord.astype(jnp.float32)
        dist = state["loc_x"] - coord_f - 0.5
        value = jnp.exp(-dist * dist / (2.0 * spread_cells * spread_cells))
        inside = (coord >= 0) & (coord < total_x)
        reach = jnp.where(inside, float(RADIUS), -1.0)
        weight = jnp.where(jnp.abs(state["cell_x"] - coord_f) <= reach, value, 0.0)
        state["sum_x"] = weight if state["sum_x"] is None else state["sum_x"] + weight
        for f in range(FIELDS):
            base = (f * CELL_X + a % CELL_X) * grid_y
            inner = None
            for b in range(grid_y):
                term = table_ref[line, base + b] * state["weight_y"][b]
                inner = term if inner is None else inner + term
            term = inner * weight
            numer = state["numer"]
            numer[f] = term if numer[f] is None else numer[f] + term

    def end():
        denom = state["sum_x"] * state["sum_y"]
        result["fields"] = [n / denom for n in state["numer"]]
        result["loc"] = (state["loc_x"], state["loc_y"])

    columns = range(CELL_X - RADIUS, 2 * CELL_X + RADIUS)
    return (
        [(100, begin)]
        + [(150, functools.partial(add_column, a)) for a in columns]
        + [(20, end)]
    )


def smooth(raw, *args):
    result = {}
    for _, piece in smooth_pieces(lambda: raw, *args, result):
        piece()
    return result["fields"], *result["loc"]


def quantities(fields, loc_x, loc_y, centre, total_x):
    first = jnp.exp(2.0 * (fields[0] + range_shift))
    second = jnp.exp(2.0 * (fields[1] + range_shift))
    cosine = jnp.cos(fields[2])
    sine = jnp.sin(fields[2])
    m_a = (cosine * cosine * first + sine * sine * second) * (1.0 / 6.0)
    m_b = (sine * sine * first + cosine * cosine * second) * (1.0 / 6.0)
    m_c = (cosine * sine * (first - second)) * (1.0 / 6.0)
    return m_a, m_b, m_c, (loc_x - centre[0]) / total_x, (loc_y - centre[1]) / total_x


def log_root(fields):
    return fields[0] + fields[1] + 2.0 * range_shift


def site_scale(fields):
    return jnp.exp(fields[3] + 0.5 * log_root(fields)) * (3.0**-0.5)


def scaled_nugget(fields):
    return (3.0 * nugget_share) * jnp.exp(-log_root(fields))


def rows_of(quant):
    a, b, c, x, y = quant
    one = jnp.ones_like(a)
    own = b * x * x + a * y * y - 2.0 * c * x * y
    return [
        one,
        own,
        b,
        a,
        c,
        x * x,
        y * y,
        x * y,
        2.0 * (c * y - b * x),
        2.0 * (c * x - a * y),
        x,
        y,
        a * b - c * c,
    ]


def form_of(quant, weight):
    a, b, c, x, y = quant
    own = b * x * x + a * y * y - 2.0 * c * x * y
    values = [
        own,
        None,
        x * x,
        y * y,
        -2.0 * x * y,
        b,
        a,
        -2.0 * c,
        x,
        y,
        2.0 * (c * y - b * x),
        2.0 * (c * x - a * y),
    ]
    return [weight if v is None else v * weight for v in values]


def det_of(quant, weight):
    a, b, c, _, _ = quant
    values = [a * b - c * c, None, b, a, -2.0 * c]
    values = [v if v is None else v * weight for v in values]
    return {0: values[0], 2: values[3], 3: values[2], 4: values[4], 12: weight}


def thirds(values):
    high = values.astype(jnp.bfloat16)
    rest = values - high.astype(jnp.float32)
    low = rest.astype(jnp.bfloat16)
    return high, low, (rest - low.astype(jnp.float32)).astype(jnp.bfloat16)


LEFT_ORDER = (0, 0, 1, 1, 0, 2, 1, 2)
RIGHT_ORDER = (0, 1, 0, 1, 2, 0, 2, 1)


def covariance(det, form):
    inv_root = lax.rsqrt(det)
    form = jnp.maximum(form, 1e-36)
    dist = form * lax.rsqrt(form) * inv_root
    return (inv_root + inv_root * dist) * jnp.exp(-dist)


def halves(values):
    high = values.astype(jnp.bfloat16)
    return high, (values - high.astype(jnp.float32)).astype(jnp.bfloat16)


def left_parts(values):
    high, low = halves(values)
    return jnp.concatenate([high, high, low], axis=1)


def right_parts(values):
    high, low = halves(values)
    return jnp.concatenate([high, low, high], axis=0)


def dot_parts(left, right):
    return jnp.dot(left, right, preferred_element_type=jnp.float32)


def lane_copy(values, lane):
    index = jnp.full(values.shape, lane, jnp.int32)
    return jnp.take_along_axis(values, index, axis=1)


def row_copy(values, row):
    return jnp.broadcast_to(values[row : row + 1, :], values.shape)


def factor_step(m, work, lines_ref, own_ref):
    steps = BLOCK // 8
    lane = lax.broadcasted_iota(jnp.int32, (8, BLOCK), 1)
    sub = lax.broadcasted_iota(jnp.int32, (8, BLOCK), 0)
    at = 8 * m
    before = at - 8

    def row(i):
        return work[8 * i : 8 * i + 8, :]

    def set_row(i, values):
        work[8 * i : 8 * i + 8, :] = values

    def updated(values, first, lines):
        term = [lane_copy(values, first + c) * lines[c] for c in range(8)]
        total = ((term[0] + term[1]) + (term[2] + term[3])) + (
            (term[4] + term[5]) + (term[6] + term[7])
        )
        return jnp.where((lane >= first) & (lane < first + 8), 0.0, values) - total

    here = row(m)
    column = [lane_copy(here, at + c) for c in range(8)]
    if m > 0:
        if m + 1 < steps:
            past = [jnp.broadcast_to(lines_ref[c : c + 1, :], (8, BLOCK)) for c in range(8)]
            following = updated(row(m + 1), before, past)
        total = {}
        for c in range(8):
            for i in range(m + 2, steps):
                term = lane_copy(row(i), before + c) * past[c]
                total[i] = term if c == 0 else total[i] + term
        for i in range(m + 2, steps):
            gone = (lane >= before) & (lane < at)
            set_row(i, jnp.where(gone, 0.0, row(i)) - total[i])
    elif m + 1 < steps:
        following = row(m + 1)
    pivots = (lane >= at) & (lane < at + 8)
    block = jnp.where(lane - at == sub, 1.0, jnp.where(pivots, 0.0, here))
    solved = jnp.zeros((8, BLOCK), jnp.float32)
    pairs = []
    for c in range(0, 8, 2):
        p = row_copy(column[c], c)
        r = row_copy(column[c + 1], c)
        q = row_copy(column[c + 1], c + 1)
        det = p * q - r * r
        inv = 1.0 / det
        both = (sub == c) | (sub == c + 1)
        first = jnp.where(both, 0.0, column[c])
        second = jnp.where(both, 0.0, column[c + 1])
        left = q * first - r * second
        right = p * second - r * first
        upper = row_copy(block, c)
        under = row_copy(block, c + 1)
        solved = jnp.where(sub == c, upper * lax.rsqrt(p), solved)
        solved = jnp.where(sub == c + 1, (p * under - r * upper) * lax.rsqrt(p * det), solved)
        pairs.append((p, r, q, inv))
        if c + 2 < 8:
            left_inv = left * inv
            right_inv = right * inv
            for j in range(c + 2, 8):
                a = row_copy(column[j], c)
                b = row_copy(column[j], c + 1)
                if j < c + 4:
                    column[j] = column[j] - (left * a + right * b) * inv
                else:
                    column[j] = (column[j] - left_inv * a) - right_inv * b
            block = (block - left_inv * upper) - right_inv * under
        else:
            block = block - (left * upper + right * under) * inv
    own_ref[at : at + 8, :] = jnp.where(lane <= at + sub, solved, 0.0)
    if m == steps - 1:
        return
    lines = []
    for h, (p, r, q, inv) in enumerate(pairs):
        upper = row_copy(block, 2 * h)
        under = row_copy(block, 2 * h + 1)
        lines.append((q * upper - r * under) * inv)
        lines.append((p * under - r * upper) * inv)
    set_row(m + 1, updated(following, at, lines))
    for c in range(8):
        lines_ref[c : c + 1, :] = lines[c][c : c + 1, :]


def at(block):
    return slice(block * BLOCK, (block + 1) * BLOCK)


def main_kernel(rows_mesh, cols, tile_ref, table_ref, buf_ref, *refs):
    packs = refs[:cols]
    (
        panel_ref,
        fields_ref,
        raws,
        nugget,
        scales,
        feats,
        panel_left,
        panel_det,
        panel_form,
        site_feats,
        site_det,
        site_form,
        gram,
        owns,
        lower,
        left,
        right,
        operand,
        work,
        lines_ref,
        residual,
        solved,
        raw_sems,
        sems,
    ) = refs[cols:]
    row = lax.axis_index("row")
    col = lax.axis_index("col")
    grid_y = cols * CELL_Y
    total_x = float(CELL_X * rows_mesh)
    width = TILE // cols
    tile = tile_ref[...][0, 0]
    start = tile * TILE
    root_row = start // (SITE_DEV * cols)
    blocks = TILE // BLOCK
    sites = cols * SITE_DEV
    chunks = sites // CHUNK
    site_lines = sites // LANES
    steps = BLOCK // 8
    lane = lax.broadcasted_iota(jnp.int32, (8, BLOCK), 1)
    sub = lax.broadcasted_iota(jnp.int32, (8, BLOCK), 0)
    centre = (
        (root_row * CELL_X).astype(jnp.float32) + 0.5 * CELL_X,
        0.5 * grid_y,
    )

    def raw_copy(k):
        return pltpu.make_async_copy(packs[k].at[0:RAW], raws.at[k], raw_sems.at[k])

    for k in range(cols):
        raw_copy(k).start()

    raw = [buf_ref[q * TILE_ROWS : (q + 1) * TILE_ROWS, :] for q in range(3)]
    fields, loc_x, loc_y = smooth(raw, root_row, table_ref, rows_mesh, grid_y)
    quant = quantities(fields, loc_x, loc_y, centre, total_x)
    nugget[...] = scaled_nugget(fields)
    one = jnp.ones_like(quant[0])
    feats[...] = jnp.zeros(feats.shape, jnp.float32)
    for n, values in enumerate((rows_of(quant), form_of(quant, one), det_of(quant, one))):
        values = values if isinstance(values, dict) else dict(enumerate(values))
        for f, value in values.items():
            for g in range(TILE_ROWS):
                feats[n, f : f + 1, g * LANES : (g + 1) * LANES] = value[g : g + 1, :]
    for k in range(cols):
        raw_copy(k).wait()

    def put_parts(target, values, lanes):
        parts = thirds(values)
        for n, part in enumerate(RIGHT_ORDER):
            target[n * FEATURES : (n + 1) * FEATURES, lanes] = parts[part]

    def panel_features(g):
        lanes = slice(g * LANES, (g + 1) * LANES)
        parts = [p.astype(jnp.float32) for p in thirds(feats[0, :, lanes])]
        stack = jnp.concatenate([parts[part] for part in LEFT_ORDER], axis=0)
        panel_left[lanes, :] = jnp.transpose(stack).astype(jnp.bfloat16)
        put_parts(panel_form, feats[1, :, lanes], lanes)
        put_parts(panel_det, feats[2, :, lanes], lanes)

    def panel_gram(i, j):
        gram[at(i), at(j)] = covariance(
            dot_parts(panel_left[at(i), :], panel_det[:, at(j)]),
            dot_parts(panel_left[at(i), :], panel_form[:, at(j)]),
        )

    def site_rows():
        raw = [
            jnp.concatenate(
                [raws[k, q * SITE_ROWS : (q + 1) * SITE_ROWS, :] for k in range(cols)], axis=0
            )
            for q in range(3)
        ]
        fields, loc_x, loc_y = smooth(raw, row, table_ref, rows_mesh, grid_y)
        for f in range(FIELDS):
            for j in range(SITE_ROWS):
                fields_ref[f : f + 1, j * LANES : (j + 1) * LANES] = fields[f][j : j + 1, :]
        quant = quantities(fields, loc_x, loc_y, centre, total_x)
        scale = site_scale(fields)
        inverse = 1.0 / scale
        weight = inverse * inverse
        site_feats[...] = jnp.zeros(site_feats.shape, jnp.float32)
        for k in range(cols):
            member = jnp.bitwise_xor(col, k) * SITE_ROWS
            mine = slice(k * SITE_ROWS, (k + 1) * SITE_ROWS)
            scales[pl.ds(pl.multiple_of(member, 8), SITE_ROWS), :] = scale[mine, :]
            for n, values in enumerate((form_of(quant, weight), det_of(quant, weight))):
                values = values if isinstance(values, dict) else dict(enumerate(values))
                for f, value in values.items():
                    for j in range(SITE_ROWS):
                        there = pl.multiple_of((member + j) * LANES, LANES)
                        at_row = k * SITE_ROWS + j
                        site_feats[n, f : f + 1, pl.ds(there, LANES)] = value[
                            at_row : at_row + 1, :
                        ]

    def site_parts(line):
        lanes = slice(line * LANES, (line + 1) * LANES)
        put_parts(site_form, site_feats[0, :, lanes], lanes)
        put_parts(site_det, site_feats[1, :, lanes], lanes)

    def copy_out(b, part):
        there = slice(b * BLOCK % width, b * BLOCK % width + BLOCK)
        return pltpu.make_async_copy(
            solved.at[at(b), part], panel_ref.at[there, part], sems.at[b]
        )

    def wide(j):
        return slice(3 * j * BLOCK, 3 * (j + 1) * BLOCK)

    def chunk_of(ch):
        return slice(ch * CHUNK, (ch + 1) * CHUNK)

    taken = set()
    fresh = set()

    def fresh_line(k, line):
        lanes = slice(line * LANES, (line + 1) * LANES)
        value = covariance(
            dot_parts(panel_left[at(k), :], site_det[:, lanes]),
            dot_parts(panel_left[at(k), :], site_form[:, lanes]),
        )
        fresh.add((k, line))
        if (k, line) in taken:
            value = value + residual[k % 2, :, lanes]
        residual[k % 2, :, lanes] = value

    def take_solved(k, ch):
        values = dot_parts(left[at(k), : 3 * k * BLOCK], right[: 3 * k * BLOCK, chunk_of(ch)])
        for p in range(CHUNK // LANES):
            line = ch * (CHUNK // LANES) + p
            lanes = slice(line * LANES, (line + 1) * LANES)
            part = values[:, p * LANES : (p + 1) * LANES]
            taken.add((k, line))
            residual[k % 2, :, lanes] = (
                residual[k % 2, :, lanes] - part if (k, line) in fresh else -part
            )

    def split_residual(k, ch):
        operand[ch % 2] = right_parts(residual[k % 2, :, chunk_of(ch)])

    def solve_chunk(k, ch):
        solved[at(k), chunk_of(ch)] = dot_parts(left[at(k), wide(k)], operand[ch % 2])

    def split_solved(k, ch):
        right[wide(k), chunk_of(ch)] = right_parts(solved[at(k), chunk_of(ch)])

    def lower_block(i, k):
        values = dot_t(gram[at(i), at(k)], owns[k])
        lower[at(i), at(k)] = values
        left[at(i), wide(k)] = left_parts(values)

    def update_block(i, j, k):
        gram[at(i), at(j)] = gram[at(i), at(j)] - dot_t(lower[at(i), at(k)], lower[at(j), at(k)])

    bounds = iter(range(0, -1000, -1))

    def stretch(code):
        pl.when(tile >= next(bounds))(code)

    def shared(count, m):
        return [n for n in range(count) if n * steps // count == m]

    def beside(k, m):
        if k == 0:
            pairs = [(i, j) for i in range(1, blocks) for j in range(i + 1)]
            if m == 0:
                for g in range(1, TILE_ROWS):
                    panel_features(g)
            for n in shared(len(pairs), m - 1) if m > 0 else ():
                panel_gram(*pairs[n])
            for line in shared(site_lines, m):
                site_parts(line)
            for line in shared(site_lines, m - 1) if m > 0 else ():
                fresh_line(0, line)
            return
        others = [(i, j) for i in range(k + 1, blocks) for j in range(k, i + 1)]
        if 0 < m <= len(others):
            update_block(*others[m - 1], k - 1)
        for line in shared(site_lines, m):
            fresh_line(k, line)
        period = steps // chunks
        ch = m // period
        if m % period == 0:
            if m == 0:
                split_residual(k - 1, 0)
            solve_chunk(k - 1, ch)
        if m % period == period - 1:
            if ch + 1 < chunks:
                split_residual(k - 1, ch + 1)
            split_solved(k - 1, ch)
            if ch > 0:
                take_solved(k, ch - 1)

    def beside_update(k):
        if k == 0:
            for line in shared(site_lines, steps - 1):
                fresh_line(0, line)
            return
        take_solved(k, chunks - 1)

    site_rows()
    panel_features(0)
    panel_gram(0, 0)
    for k in range(blocks):

        for first in range(0, steps, STRETCH):

            @stretch
            def _(k=k, first=first):
                for i in range(steps) if first == 0 else ():
                    rows = slice(8 * i, 8 * i + 8)
                    values = gram[k * BLOCK + 8 * i : k * BLOCK + 8 * i + 8, at(k)]
                    nug = jnp.broadcast_to(nugget[k : k + 1, :], (8, BLOCK))
                    work[rows, :] = values + jnp.where(lane - 8 * i == sub, nug, 0.0)
                for m in range(first, first + STRETCH):
                    factor_step(m, work, lines_ref, owns.at[k])
                    beside(k, m)

        @stretch
        def _(k=k):
            if k + 1 < blocks:
                lower_block(k + 1, k)
                update_block(k + 1, k + 1, k)
            for i in range(k + 2, blocks):
                lower_block(i, k)
            left[at(k), wide(k)] = left_parts(owns[k])
            beside_update(k)

        if k > 0:

            @pl.when(col == (k - 1) * BLOCK // width)
            def _(k=k):
                copy_out(k - 1, slice(None)).start()

        offset = start + k * BLOCK - row * sites

        @pl.when((offset >= 0) & (offset < sites))
        def _(k=k, offset=offset):
            nug = nugget[k : k + 1, :] * scales[pl.ds(offset // LANES, 1), :]
            here = pl.ds(pl.multiple_of(offset, LANES), LANES)
            for i in range(steps):
                rows = slice(8 * i, 8 * i + 8)
                residual[k % 2, rows, here] = residual[k % 2, rows, here] + jnp.where(
                    lane - 8 * i == sub, jnp.broadcast_to(nug, (8, LANES)), 0.0
                )

    last = blocks - 1
    mine = col == last * BLOCK // width
    for ch in range(chunks):
        part = slice(ch * CHUNK, (ch + 1) * CHUNK)
        split_residual(last, ch)
        solve_chunk(last, ch)

        @pl.when(mine)
        def _(part=part):
            copy_out(last, part).start()

    for b in range(blocks):

        @pl.when(col == b * BLOCK // width)
        def _(b=b):
            copy_out(b, slice(None)).wait()


def body(offsets, site_cell, estimates, panel_tile):
    rows_mesh = lax.axis_size("row")
    cols = lax.axis_size("col")
    devices = rows_mesh * cols
    assert FIELDS * CELL_X * CELL_Y * cols == LANES
    assert devices & (devices - 1) == 0
    vmem = pl.BlockSpec(memory_space=pltpu.VMEM)
    smem = pl.BlockSpec(memory_space=pltpu.SMEM)
    pack = pl.pallas_call(
        functools.partial(pack_kernel, cols),
        out_shape=pltpu.VMEM((RAW + HEAD + rows_mesh, LANES), jnp.float32),
        in_specs=[vmem, smem, vmem, vmem],
        out_specs=vmem,
    )(panel_tile.reshape(1, 1), estimates, offsets, site_cell.reshape(1, -1))
    packs = [pack]
    buf = pack[RAW:]
    step = 1
    while step < cols:
        pairs = [(i, i ^ step) for i in range(devices)]
        sent = jnp.concatenate([pack[:RAW], buf], axis=0) if step > 1 else pack
        near = lax.ppermute(sent, ("row", "col"), pairs)
        far = [lax.ppermute(packs[k], ("row", "col"), pairs) for k in range(1, step)]
        packs += [near] + far
        buf = buf + near[RAW:]
        step *= 2
    bits = []
    while step < devices:
        bits.append(step)
        step *= 2
    half = (len(bits) + 1) // 2
    order = [n for pair in zip(bits[:half], bits[half:]) for n in pair] + bits[len(bits) // 2 : half]
    for n in range(len(order)):
        other = order[n ^ 1] if (n ^ 1) < len(order) else order[n]
        pairs = [(i, i ^ (other if i % cols % 2 else order[n])) for i in range(devices)]
        buf = buf + lax.ppermute(buf, ("row", "col"), pairs)
    width = TILE // cols
    sites = cols * SITE_DEV
    anywhere = pl.BlockSpec(memory_space=pl.ANY)
    panel, fields = pl.pallas_call(
        functools.partial(main_kernel, rows_mesh, cols),
        out_shape=(
            jax.ShapeDtypeStruct((width, sites), jnp.float32),
            jax.ShapeDtypeStruct((FIELDS, SITE_DEV), jnp.float32),
        ),
        in_specs=[vmem, smem, vmem] + [anywhere] * cols,
        out_specs=(anywhere, vmem),
        scratch_shapes=[
            pltpu.VMEM((cols, RAW, LANES), jnp.float32),
            pltpu.VMEM((TILE_ROWS, LANES), jnp.float32),
            pltpu.VMEM((cols * SITE_ROWS, LANES), jnp.float32),
            pltpu.VMEM((3, FEATURES, TILE), jnp.float32),
            pltpu.VMEM((TILE, COPIES * FEATURES), jnp.bfloat16),
            pltpu.VMEM((COPIES * FEATURES, TILE), jnp.bfloat16),
            pltpu.VMEM((COPIES * FEATURES, TILE), jnp.bfloat16),
            pltpu.VMEM((2, FEATURES, sites), jnp.float32),
            pltpu.VMEM((COPIES * FEATURES, sites), jnp.bfloat16),
            pltpu.VMEM((COPIES * FEATURES, sites), jnp.bfloat16),
            pltpu.VMEM((TILE, TILE), jnp.float32),
            pltpu.VMEM((TILE // BLOCK, BLOCK, BLOCK), jnp.float32),
            pltpu.VMEM((TILE, TILE), jnp.float32),
            pltpu.VMEM((TILE, 3 * TILE), jnp.bfloat16),
            pltpu.VMEM((3 * (TILE - BLOCK), sites), jnp.bfloat16),
            pltpu.VMEM((2, 3 * BLOCK, CHUNK), jnp.bfloat16),
            pltpu.VMEM((BLOCK, BLOCK), jnp.float32),
            pltpu.VMEM((8, BLOCK), jnp.float32),
            pltpu.VMEM((2, BLOCK, sites), jnp.float32),
            pltpu.VMEM((TILE, sites), jnp.float32),
            pltpu.SemaphoreType.DMA((cols,)),
            pltpu.SemaphoreType.DMA((TILE // BLOCK,)),
        ],
        compiler_params=pltpu.CompilerParams(
            vmem_limit_bytes=40 * 1024 * 1024,
        ),
    )(panel_tile.reshape(1, 1), buf, buf, *packs)
    return (panel, fields)


def solution(mesh):
    placed = (P(None, ("row", "col")), P(("row", "col")), P(None, "row", "col"), P())
    return jax.shard_map(
        body,
        mesh=mesh,
        in_specs=placed,
        out_specs=(P("col", "row"), P(None, ("row", "col"))),
        check_vma=False,
    )
```

```python
import functools

import jax
import jax.numpy as jnp
from jax import lax
from jax.experimental import pallas as pl
from jax.experimental.pallas import tpu as pltpu
from jax.sharding import PartitionSpec as P

SITE_DEV = 1024
TILE = 512
CELL_X = 4
CELL_Y = 4
RADIUS = 2

spread_cells = 1.5
nugget_share = 0.5
range_shift = -0.7

LANES = 128
BLOCK = 128
FIELDS = 4
SITE_ROWS = SITE_DEV // LANES
TILE_ROWS = TILE // LANES
RAW = 3 * SITE_ROWS
HEAD = 3 * TILE_ROWS
CHUNK = 256
STRETCH = 4
FEATURES = 16
COPIES = 8

HIGHEST = lax.Precision.HIGHEST


def dot(a, b):
    return jnp.dot(a, b, precision=HIGHEST, preferred_element_type=jnp.float32)


def dot_t(a, b):
    return lax.dot_general(
        a, b, (((1,), (1,)), ((), ())), precision=HIGHEST, preferred_element_type=jnp.float32
    )


def pack_kernel(cols, tile_ref, est_ref, offsets_ref, cell_ref, out_ref):
    row = lax.axis_index("row")
    col = lax.axis_index("col")
    for j in range(SITE_ROWS):
        part = slice(j * LANES, (j + 1) * LANES)
        out_ref[j : j + 1, :] = offsets_ref[0:1, part]
        out_ref[SITE_ROWS + j : SITE_ROWS + j + 1, :] = offsets_ref[1:2, part]
        out_ref[2 * SITE_ROWS + j : 2 * SITE_ROWS + j + 1, :] = cell_ref[0:1, part].astype(
            jnp.float32
        )
    start = tile_ref[...][0, 0] * TILE
    root = start // SITE_DEV
    first = (start - root * SITE_DEV) // LANES
    mine = row * cols + col == root
    for q in range(3):
        rows = out_ref[pl.ds(q * SITE_ROWS + first, TILE_ROWS), :]
        there = RAW + q * TILE_ROWS
        out_ref[there : there + TILE_ROWS, :] = jnp.where(mine, rows, 0.0)
    grid_y = cols * CELL_Y
    lane = lax.broadcasted_iota(jnp.int32, (1, LANES), 1) - col * CELL_Y
    terms = []
    for f in range(FIELDS):
        for a in range(CELL_X):
            line = jnp.zeros((1, LANES), jnp.float32)
            for b in range(CELL_Y):
                line = jnp.where(
                    lane == (f * CELL_X + a) * grid_y + b, est_ref[f, a, b], line
                )
            terms.append(line)
    while len(terms) > 1:
        terms = [x + y for x, y in zip(terms[::2], terms[1::2])]
    count = out_ref.shape[0] - RAW - HEAD
    index = lax.broadcasted_iota(jnp.int32, (count, LANES), 0)
    out_ref[RAW + HEAD :, :] = jnp.where(
        index == row, jnp.broadcast_to(terms[0], (count, LANES)), 0.0
    )


def smooth_pieces(get_raw, block_row, table_ref, rows_mesh, grid_y, result):
    total_x = CELL_X * rows_mesh
    state = {"numer": [None] * FIELDS, "sum_x": None}

    def begin():
        off_x, off_y, cell = get_raw()
        cell_x = jnp.floor((cell + 0.5) / grid_y)
        cell_y = cell - cell_x * grid_y
        state.update(cell_x=cell_x, loc_x=cell_x + off_x, loc_y=cell_y + off_y)
        weight_y = []
        for b in range(grid_y):
            dist = state["loc_y"] - (b + 0.5)
            value = jnp.exp(-dist * dist / (2.0 * spread_cells * spread_cells))
            weight_y.append(jnp.where(jnp.abs(cell_y - b) <= RADIUS, value, 0.0))
        state.update(weight_y=weight_y, sum_y=functools.reduce(jnp.add, weight_y))

    def add_column(a):
        coord = (block_row - 1) * CELL_X + a
        near = block_row - 1 + a // CELL_X
        line = HEAD + jnp.clip(near, 0, rows_mesh - 1)
        coord_f = coord.astype(jnp.float32)
        dist = state["loc_x"] - coord_f - 0.5
        value = jnp.exp(-dist * dist / (2.0 * spread_cells * spread_cells))
        inside = (coord >= 0) & (coord < total_x)
        reach = jnp.where(inside, float(RADIUS), -1.0)
        weight = jnp.where(jnp.abs(state["cell_x"] - coord_f) <= reach, value, 0.0)
        state["sum_x"] = weight if state["sum_x"] is None else state["sum_x"] + weight
        for f in range(FIELDS):
            base = (f * CELL_X + a % CELL_X) * grid_y
            inner = None
            for b in range(grid_y):
                term = table_ref[line, base + b] * state["weight_y"][b]
                inner = term if inner is None else inner + term
            term = inner * weight
            numer = state["numer"]
            numer[f] = term if numer[f] is None else numer[f] + term

    def end():
        denom = state["sum_x"] * state["sum_y"]
        result["fields"] = [n / denom for n in state["numer"]]
        result["loc"] = (state["loc_x"], state["loc_y"])

    columns = range(CELL_X - RADIUS, 2 * CELL_X + RADIUS)
    return (
        [(100, begin)]
        + [(150, functools.partial(add_column, a)) for a in columns]
        + [(20, end)]
    )


def smooth(raw, *args):
    result = {}
    for _, piece in smooth_pieces(lambda: raw, *args, result):
        piece()
    return result["fields"], *result["loc"]


def quantities(fields, loc_x, loc_y, centre, total_x):
    first = jnp.exp(2.0 * (fields[0] + range_shift))
    second = jnp.exp(2.0 * (fields[1] + range_shift))
    cosine = jnp.cos(fields[2])
    sine = jnp.sin(fields[2])
    m_a = (cosine * cosine * first + sine * sine * second) * (1.0 / 6.0)
    m_b = (sine * sine * first + cosine * cosine * second) * (1.0 / 6.0)
    m_c = (cosine * sine * (first - second)) * (1.0 / 6.0)
    return m_a, m_b, m_c, (loc_x - centre[0]) / total_x, (loc_y - centre[1]) / total_x


def log_root(fields):
    return fields[0] + fields[1] + 2.0 * range_shift


def site_scale(fields):
    return jnp.exp(fields[3] + 0.5 * log_root(fields)) * (3.0**-0.5)


def scaled_nugget(fields):
    return (3.0 * nugget_share) * jnp.exp(-log_root(fields))


def rows_of(quant):
    a, b, c, x, y = quant
    one = jnp.ones_like(a)
    own = b * x * x + a * y * y - 2.0 * c * x * y
    return [
        one,
        own,
        b,
        a,
        c,
        x * x,
        y * y,
        x * y,
        2.0 * (c * y - b * x),
        2.0 * (c * x - a * y),
        x,
        y,
        a * b - c * c,
    ]


def form_of(quant, weight):
    a, b, c, x, y = quant
    own = b * x * x + a * y * y - 2.0 * c * x * y
    values = [
        own,
        None,
        x * x,
        y * y,
        -2.0 * x * y,
        b,
        a,
        -2.0 * c,
        x,
        y,
        2.0 * (c * y - b * x),
        2.0 * (c * x - a * y),
    ]
    return [weight if v is None else v * weight for v in values]


def det_of(quant, weight):
    a, b, c, _, _ = quant
    values = [a * b - c * c, None, b, a, -2.0 * c]
    values = [v if v is None else v * weight for v in values]
    return {0: values[0], 2: values[3], 3: values[2], 4: values[4], 12: weight}


def thirds(values):
    high = values.astype(jnp.bfloat16)
    rest = values - high.astype(jnp.float32)
    low = rest.astype(jnp.bfloat16)
    return high, low, (rest - low.astype(jnp.float32)).astype(jnp.bfloat16)


LEFT_ORDER = (0, 0, 1, 1, 0, 2, 1, 2)
RIGHT_ORDER = (0, 1, 0, 1, 2, 0, 2, 1)


def covariance(det, form):
    inv_root = lax.rsqrt(det)
    form = jnp.maximum(form, 1e-36)
    dist = form * lax.rsqrt(form) * inv_root
    return (inv_root + inv_root * dist) * jnp.exp(-dist)


def halves(values):
    high = values.astype(jnp.bfloat16)
    return high, (values - high.astype(jnp.float32)).astype(jnp.bfloat16)


def left_parts(values):
    high, low = halves(values)
    return jnp.concatenate([high, high, low], axis=1)


def right_parts(values):
    high, low = halves(values)
    return jnp.concatenate([high, low, high], axis=0)


def dot_parts(left, right):
    return jnp.dot(left, right, preferred_element_type=jnp.float32)


def lane_copy(values, lane):
    index = jnp.full(values.shape, lane, jnp.int32)
    return jnp.take_along_axis(values, index, axis=1)


def row_copy(values, row):
    return jnp.broadcast_to(values[row : row + 1, :], values.shape)


def factor_step(m, work, lines_ref, own_ref):
    steps = BLOCK // 8
    lane = lax.broadcasted_iota(jnp.int32, (8, BLOCK), 1)
    sub = lax.broadcasted_iota(jnp.int32, (8, BLOCK), 0)
    at = 8 * m
    before = at - 8

    def row(i):
        return work[8 * i : 8 * i + 8, :]

    def set_row(i, values):
        work[8 * i : 8 * i + 8, :] = values

    def updated(values, first, lines):
        term = [lane_copy(values, first + c) * lines[c] for c in range(8)]
        total = ((term[0] + term[1]) + (term[2] + term[3])) + (
            (term[4] + term[5]) + (term[6] + term[7])
        )
        return jnp.where((lane >= first) & (lane < first + 8), 0.0, values) - total

    here = row(m)
    column = [lane_copy(here, at + c) for c in range(8)]
    if m > 0:
        if m + 1 < steps:
            past = [jnp.broadcast_to(lines_ref[c : c + 1, :], (8, BLOCK)) for c in range(8)]
            following = updated(row(m + 1), before, past)
        total = {}
        for c in range(8):
            for i in range(m + 2, steps):
                term = lane_copy(row(i), before + c) * past[c]
                total[i] = term if c == 0 else total[i] + term
        for i in range(m + 2, steps):
            gone = (lane >= before) & (lane < at)
            set_row(i, jnp.where(gone, 0.0, row(i)) - total[i])
    elif m + 1 < steps:
        following = row(m + 1)
    pivots = (lane >= at) & (lane < at + 8)
    block = jnp.where(lane - at == sub, 1.0, jnp.where(pivots, 0.0, here))
    solved = jnp.zeros((8, BLOCK), jnp.float32)
    pairs = []
    for c in range(0, 8, 2):
        p = row_copy(column[c], c)
        r = row_copy(column[c + 1], c)
        q = row_copy(column[c + 1], c + 1)
        det = p * q - r * r
        inv = 1.0 / det
        both = (sub == c) | (sub == c + 1)
        first = jnp.where(both, 0.0, column[c])
        second = jnp.where(both, 0.0, column[c + 1])
        left = q * first - r * second
        right = p * second - r * first
        upper = row_copy(block, c)
        under = row_copy(block, c + 1)
        solved = jnp.where(sub == c, upper * lax.rsqrt(p), solved)
        solved = jnp.where(sub == c + 1, (p * under - r * upper) * lax.rsqrt(p * det), solved)
        pairs.append((p, r, q, inv))
        if c + 2 < 8:
            left_inv = left * inv
            right_inv = right * inv
            for j in range(c + 2, 8):
                a = row_copy(column[j], c)
                b = row_copy(column[j], c + 1)
                if j < c + 4:
                    column[j] = column[j] - (left * a + right * b) * inv
                else:
                    column[j] = (column[j] - left_inv * a) - right_inv * b
            block = (block - left_inv * upper) - right_inv * under
        else:
            block = block - (left * upper + right * under) * inv
    own_ref[at : at + 8, :] = jnp.where(lane <= at + sub, solved, 0.0)
    if m == steps - 1:
        return
    lines = []
    for h, (p, r, q, inv) in enumerate(pairs):
        upper = row_copy(block, 2 * h)
        under = row_copy(block, 2 * h + 1)
        lines.append((q * upper - r * under) * inv)
        lines.append((p * under - r * upper) * inv)
    set_row(m + 1, updated(following, at, lines))
    for c in range(8):
        lines_ref[c : c + 1, :] = lines[c][c : c + 1, :]


def at(block):
    return slice(block * BLOCK, (block + 1) * BLOCK)


def main_kernel(rows_mesh, cols, tile_ref, table_ref, buf_ref, *refs):
    packs = refs[:cols]
    (
        panel_ref,
        fields_ref,
        raws,
        nugget,
        scales,
        feats,
        panel_left,
        panel_det,
        panel_form,
        site_feats,
        site_det,
        site_form,
        gram,
        owns,
        lower,
        left,
        right,
        operand,
        work,
        lines_ref,
        residual,
        solved,
        raw_sems,
        sems,
    ) = refs[cols:]
    row = lax.axis_index("row")
    col = lax.axis_index("col")
    grid_y = cols * CELL_Y
    total_x = float(CELL_X * rows_mesh)
    width = TILE // cols
    tile = tile_ref[...][0, 0]
    start = tile * TILE
    root_row = start // (SITE_DEV * cols)
    blocks = TILE // BLOCK
    sites = cols * SITE_DEV
    chunks = sites // CHUNK
    site_lines = sites // LANES
    steps = BLOCK // 8
    lane = lax.broadcasted_iota(jnp.int32, (8, BLOCK), 1)
    sub = lax.broadcasted_iota(jnp.int32, (8, BLOCK), 0)
    centre = (
        (root_row * CELL_X).astype(jnp.float32) + 0.5 * CELL_X,
        0.5 * grid_y,
    )

    def raw_copy(k):
        return pltpu.make_async_copy(packs[k].at[0:RAW], raws.at[k], raw_sems.at[k])

    for k in range(cols):
        raw_copy(k).start()

    raw = [buf_ref[q * TILE_ROWS : (q + 1) * TILE_ROWS, :] for q in range(3)]
    fields, loc_x, loc_y = smooth(raw, root_row, table_ref, rows_mesh, grid_y)
    quant = quantities(fields, loc_x, loc_y, centre, total_x)
    nugget[...] = scaled_nugget(fields)
    one = jnp.ones_like(quant[0])
    feats[...] = jnp.zeros(feats.shape, jnp.float32)
    for n, values in enumerate((rows_of(quant), form_of(quant, one), det_of(quant, one))):
        values = values if isinstance(values, dict) else dict(enumerate(values))
        for f, value in values.items():
            for g in range(TILE_ROWS):
                feats[n, f : f + 1, g * LANES : (g + 1) * LANES] = value[g : g + 1, :]
    for k in range(cols):
        raw_copy(k).wait()

    def put_parts(target, values, lanes):
        parts = thirds(values)
        for n, part in enumerate(RIGHT_ORDER):
            target[n * FEATURES : (n + 1) * FEATURES, lanes] = parts[part]

    def panel_features(g):
        lanes = slice(g * LANES, (g + 1) * LANES)
        parts = [p.astype(jnp.float32) for p in thirds(feats[0, :, lanes])]
        stack = jnp.concatenate([parts[part] for part in LEFT_ORDER], axis=0)
        panel_left[lanes, :] = jnp.transpose(stack).astype(jnp.bfloat16)
        put_parts(panel_form, feats[1, :, lanes], lanes)
        put_parts(panel_det, feats[2, :, lanes], lanes)

    def panel_gram(i, j):
        gram[at(i), at(j)] = covariance(
            dot_parts(panel_left[at(i), :], panel_det[:, at(j)]),
            dot_parts(panel_left[at(i), :], panel_form[:, at(j)]),
        )

    def site_rows():
        raw = [
            jnp.concatenate(
                [raws[k, q * SITE_ROWS : (q + 1) * SITE_ROWS, :] for k in range(cols)], axis=0
            )
            for q in range(3)
        ]
        fields, loc_x, loc_y = smooth(raw, row, table_ref, rows_mesh, grid_y)
        for f in range(FIELDS):
            for j in range(SITE_ROWS):
                fields_ref[f : f + 1, j * LANES : (j + 1) * LANES] = fields[f][j : j + 1, :]
        quant = quantities(fields, loc_x, loc_y, centre, total_x)
        scale = site_scale(fields)
        inverse = 1.0 / scale
        weight = inverse * inverse
        site_feats[...] = jnp.zeros(site_feats.shape, jnp.float32)
        for k in range(cols):
            member = jnp.bitwise_xor(col, k) * SITE_ROWS
            mine = slice(k * SITE_ROWS, (k + 1) * SITE_ROWS)
            scales[pl.ds(pl.multiple_of(member, 8), SITE_ROWS), :] = scale[mine, :]
            for n, values in enumerate((form_of(quant, weight), det_of(quant, weight))):
                values = values if isinstance(values, dict) else dict(enumerate(values))
                for f, value in values.items():
                    for j in range(SITE_ROWS):
                        there = pl.multiple_of((member + j) * LANES, LANES)
                        at_row = k * SITE_ROWS + j
                        site_feats[n, f : f + 1, pl.ds(there, LANES)] = value[
                            at_row : at_row + 1, :
                        ]

    def site_parts(line):
        lanes = slice(line * LANES, (line + 1) * LANES)
        put_parts(site_form, site_feats[0, :, lanes], lanes)
        put_parts(site_det, site_feats[1, :, lanes], lanes)

    def copy_out(b, part):
        there = slice(b * BLOCK % width, b * BLOCK % width + BLOCK)
        return pltpu.make_async_copy(
            solved.at[at(b), part], panel_ref.at[there, part], sems.at[b]
        )

    def wide(j):
        return slice(3 * j * BLOCK, 3 * (j + 1) * BLOCK)

    def chunk_of(ch):
        return slice(ch * CHUNK, (ch + 1) * CHUNK)

    taken = set()
    fresh = set()

    def fresh_line(k, line):
        lanes = slice(line * LANES, (line + 1) * LANES)
        value = covariance(
            dot_parts(panel_left[at(k), :], site_det[:, lanes]),
            dot_parts(panel_left[at(k), :], site_form[:, lanes]),
        )
        fresh.add((k, line))
        if (k, line) in taken:
            value = value + residual[k % 2, :, lanes]
        residual[k % 2, :, lanes] = value

    def take_solved(k, ch):
        values = dot_parts(left[at(k), : 3 * k * BLOCK], right[: 3 * k * BLOCK, chunk_of(ch)])
        for p in range(CHUNK // LANES):
            line = ch * (CHUNK // LANES) + p
            lanes = slice(line * LANES, (line + 1) * LANES)
            part = values[:, p * LANES : (p + 1) * LANES]
            taken.add((k, line))
            residual[k % 2, :, lanes] = (
                residual[k % 2, :, lanes] - part if (k, line) in fresh else -part
            )

    def split_residual(k, ch):
        operand[ch % 2] = right_parts(residual[k % 2, :, chunk_of(ch)])

    def solve_chunk(k, ch):
        solved[at(k), chunk_of(ch)] = dot_parts(left[at(k), wide(k)], operand[ch % 2])

    def split_solved(k, ch):
        right[wide(k), chunk_of(ch)] = right_parts(solved[at(k), chunk_of(ch)])

    def lower_block(i, k):
        values = dot_t(gram[at(i), at(k)], owns[k])
        lower[at(i), at(k)] = values
        left[at(i), wide(k)] = left_parts(values)

    def update_block(i, j, k):
        gram[at(i), at(j)] = gram[at(i), at(j)] - dot_t(lower[at(i), at(k)], lower[at(j), at(k)])

    bounds = iter(range(0, -1000, -1))

    def stretch(code):
        pl.when(tile >= next(bounds))(code)

    def shared(count, m):
        return [n for n in range(count) if n * steps // count == m]

    def beside(k, m):
        if k == 0:
            pairs = [(i, j) for i in range(1, blocks) for j in range(i + 1)]
            if m == 0:
                for g in range(1, TILE_ROWS):
                    panel_features(g)
            for n in shared(len(pairs), m - 1) if m > 0 else ():
                panel_gram(*pairs[n])
            for line in shared(site_lines, m):
                site_parts(line)
            for line in shared(site_lines, m - 1) if m > 0 else ():
                fresh_line(0, line)
            return
        others = [(i, j) for i in range(k + 1, blocks) for j in range(k, i + 1)]
        if 0 < m <= len(others):
            update_block(*others[m - 1], k - 1)
        for line in shared(site_lines, m):
            fresh_line(k, line)
        period = steps // chunks
        ch = m // period
        if m % period == 0:
            if m == 0:
                split_residual(k - 1, 0)
            solve_chunk(k - 1, ch)
        if m % period == period - 1:
            if ch + 1 < chunks:
                split_residual(k - 1, ch + 1)
            split_solved(k - 1, ch)
            if ch > 0:
                take_solved(k, ch - 1)

    def beside_update(k):
        if k == 0:
            for line in shared(site_lines, steps - 1):
                fresh_line(0, line)
            return
        take_solved(k, chunks - 1)

    site_rows()
    panel_features(0)
    panel_gram(0, 0)
    for k in range(blocks):

        for first in range(0, steps, STRETCH):

            @stretch
            def _(k=k, first=first):
                for i in range(steps) if first == 0 else ():
                    rows = slice(8 * i, 8 * i + 8)
                    values = gram[k * BLOCK + 8 * i : k * BLOCK + 8 * i + 8, at(k)]
                    nug = jnp.broadcast_to(nugget[k : k + 1, :], (8, BLOCK))
                    work[rows, :] = values + jnp.where(lane - 8 * i == sub, nug, 0.0)
                for m in range(first, first + STRETCH):
                    factor_step(m, work, lines_ref, owns.at[k])
                    beside(k, m)

        @stretch
        def _(k=k):
            if k + 1 < blocks:
                lower_block(k + 1, k)
                update_block(k + 1, k + 1, k)
            for i in range(k + 2, blocks):
                lower_block(i, k)
            left[at(k), wide(k)] = left_parts(owns[k])
            beside_update(k)

        if k > 0:

            @pl.when(col == (k - 1) * BLOCK // width)
            def _(k=k):
                copy_out(k - 1, slice(None)).start()

        offset = start + k * BLOCK - row * sites

        @pl.when((offset >= 0) & (offset < sites))
        def _(k=k, offset=offset):
            nug = nugget[k : k + 1, :] * scales[pl.ds(offset // LANES, 1), :]
            here = pl.ds(pl.multiple_of(offset, LANES), LANES)
            for i in range(steps):
                rows = slice(8 * i, 8 * i + 8)
                residual[k % 2, rows, here] = residual[k % 2, rows, here] + jnp.where(
                    lane - 8 * i == sub, jnp.broadcast_to(nug, (8, LANES)), 0.0
                )

    last = blocks - 1
    mine = col == last * BLOCK // width
    for ch in range(chunks):
        part = slice(ch * CHUNK, (ch + 1) * CHUNK)
        split_residual(last, ch)
        solve_chunk(last, ch)

        @pl.when(mine)
        def _(part=part):
            copy_out(last, part).start()

    for b in range(blocks):

        @pl.when(col == b * BLOCK // width)
        def _(b=b):
            copy_out(b, slice(None)).wait()


def body(offsets, site_cell, estimates, panel_tile):
    rows_mesh = lax.axis_size("row")
    cols = lax.axis_size("col")
    devices = rows_mesh * cols
    assert FIELDS * CELL_X * CELL_Y * cols == LANES
    assert devices & (devices - 1) == 0
    vmem = pl.BlockSpec(memory_space=pltpu.VMEM)
    smem = pl.BlockSpec(memory_space=pltpu.SMEM)
    pack = pl.pallas_call(
        functools.partial(pack_kernel, cols),
        out_shape=pltpu.VMEM((RAW + HEAD + rows_mesh, LANES), jnp.float32),
        in_specs=[vmem, smem, vmem, vmem],
        out_specs=vmem,
    )(panel_tile.reshape(1, 1), estimates, offsets, site_cell.reshape(1, -1))
    packs = [pack]
    buf = pack[RAW:]
    step = 1
    while step < cols:
        pairs = [(i, i ^ step) for i in range(devices)]
        sent = jnp.concatenate([pack[:RAW], buf], axis=0) if step > 1 else pack
        near = lax.ppermute(sent, ("row", "col"), pairs)
        far = [lax.ppermute(packs[k], ("row", "col"), pairs) for k in range(1, step)]
        packs += [near] + far
        buf = buf + near[RAW:]
        step *= 2
    while step < devices:
        pairs = [(i, i ^ step ^ (cols - 1)) for i in range(devices)]
        buf = buf + lax.ppermute(buf, ("row", "col"), pairs)
        step *= 2
    width = TILE // cols
    sites = cols * SITE_DEV
    anywhere = pl.BlockSpec(memory_space=pl.ANY)
    panel, fields = pl.pallas_call(
        functools.partial(main_kernel, rows_mesh, cols),
        out_shape=(
            jax.ShapeDtypeStruct((width, sites), jnp.float32),
            jax.ShapeDtypeStruct((FIELDS, SITE_DEV), jnp.float32),
        ),
        in_specs=[vmem, smem, vmem] + [anywhere] * cols,
        out_specs=(anywhere, vmem),
        scratch_shapes=[
            pltpu.VMEM((cols, RAW, LANES), jnp.float32),
            pltpu.VMEM((TILE_ROWS, LANES), jnp.float32),
            pltpu.VMEM((cols * SITE_ROWS, LANES), jnp.float32),
            pltpu.VMEM((3, FEATURES, TILE), jnp.float32),
            pltpu.VMEM((TILE, COPIES * FEATURES), jnp.bfloat16),
            pltpu.VMEM((COPIES * FEATURES, TILE), jnp.bfloat16),
            pltpu.VMEM((COPIES * FEATURES, TILE), jnp.bfloat16),
            pltpu.VMEM((2, FEATURES, sites), jnp.float32),
            pltpu.VMEM((COPIES * FEATURES, sites), jnp.bfloat16),
            pltpu.VMEM((COPIES * FEATURES, sites), jnp.bfloat16),
            pltpu.VMEM((TILE, TILE), jnp.float32),
            pltpu.VMEM((TILE // BLOCK, BLOCK, BLOCK), jnp.float32),
            pltpu.VMEM((TILE, TILE), jnp.float32),
            pltpu.VMEM((TILE, 3 * TILE), jnp.bfloat16),
            pltpu.VMEM((3 * (TILE - BLOCK), sites), jnp.bfloat16),
            pltpu.VMEM((2, 3 * BLOCK, CHUNK), jnp.bfloat16),
            pltpu.VMEM((BLOCK, BLOCK), jnp.float32),
            pltpu.VMEM((8, BLOCK), jnp.float32),
            pltpu.VMEM((2, BLOCK, sites), jnp.float32),
            pltpu.VMEM((TILE, sites), jnp.float32),
            pltpu.SemaphoreType.DMA((cols,)),
            pltpu.SemaphoreType.DMA((TILE // BLOCK,)),
        ],
        compiler_params=pltpu.CompilerParams(
            vmem_limit_bytes=40 * 1024 * 1024,
        ),
    )(panel_tile.reshape(1, 1), buf, buf, *packs)
    return (panel, fields)


def solution(mesh):
    placed = (P(None, ("row", "col")), P(("row", "col")), P(None, "row", "col"), P())
    return jax.shard_map(
        body,
        mesh=mesh,
        in_specs=placed,
        out_specs=(P("col", "row"), P(None, ("row", "col"))),
        check_vma=False,
    )
```
